32 devices in a mesh: wide: 16 (over z, y, x), narrow: 2 (over core).
Axes of the slice: x: 2, y: 2, z: 4, core: 2. Of those that a mesh axis runs over, the one named last changes fastest.
Arguments:
- right_side: float32 [256, 32, 128], P('wide', 'narrow'), may hold values from -8 to 8
- labels: int32 [32, 4, 16], P('wide', 'narrow'), may hold values from 0 to 15
- material_table: float32 [16], replicated, may hold values from 0.1 to 10
- robin_table: float32 [8], replicated, may hold values from 0.5 to 8
- robin_index: int32 [16, 2, 2], P('wide', 'narrow'), may hold values from 0 to 7
- coarse_rows: float32 [32, 32], P(('wide', 'narrow')), may hold values from -0.005859375 to 0.005859375
Outputs:
- solution: bfloat16 [256, 32, 128], P('wide', 'narrow')
- residual: bfloat16 [256, 32, 128], P('wide', 'narrow')
The draws below stay inside these ranges and needn't reach their ends.
All inputs are finite; a program needn't handle non-finite values.
Results may differ from the reference program's by a relative error of at most 0.0015.
Values sent between devices are 32-bit elements; how exact they have to be, the bound alone decides.
A program may use at most 64 MiB of HBM per device.

```python
import math
import jax
import jax.numpy as jnp
from jax import lax

CX = 16
CY = 16
NZ = 128
BLOCK = 8
MATERIALS = 16
ROBINS = 8
SWEEPS = 4
ITERS = 2
NX = 256
NY = 32
COARSE = 32
N_WIDE = 16
N_NARROW = 2


def place_ends(result, stream_key, low, largest):
    longest = result.shape.index(max(result.shape))
    spots = []
    for shift in (0, 1):
        where = [jax.random.randint(jax.random.fold_in(stream_key, axis), (), 0, length) for axis, length in enumerate(result.shape)]
        where[longest] = (where[longest] + shift) % result.shape[longest]
        spots.append(tuple(where))
    return result.at[spots[0]].set(low).at[spots[1]].set(largest)


def block_levels(rng, shape, split, least, top_value):
    gain = 1.0
    for dim, shards_of in split:
        heights = jax.random.uniform(jax.random.fold_in(jax.random.fold_in(rng, 6), dim), (shards_of,), jnp.float32, least / len(split), top_value / len(split))
        gain = gain * jnp.repeat(jnp.exp(heights), shape[dim] // shards_of).reshape((-1,) + (1,) * (len(shape) - 1 - dim))
    return gain


def scatter_about(stream_key, shape, deviation, bound, pieces=(), held_as=jnp.bfloat16):
    values = deviation * jax.random.normal(stream_key, shape, jnp.float32)
    if pieces:
        values = values * block_levels(stream_key, shape, pieces, -0.22, 0.18)
    return jnp.clip(values, -bound, bound).astype(held_as)


def setup_inputs(seed: int = 0) -> dict:
    key_of = jax.random.split(jax.random.key(seed), 7)
    return {
        "right_side": scatter_about(key_of[0], (NX, NY, NZ), 1.0, 8.0, ((0, 16), (1, 2)), jnp.float32),
        "labels": place_ends(jax.random.randint(key_of[1], (NX // BLOCK, NY // BLOCK, NZ // BLOCK), 0, MATERIALS), jax.random.fold_in(key_of[1], 1), 0, MATERIALS - 1).astype(jnp.int32),
        "material_table": jnp.clip(jnp.exp(jax.random.uniform(key_of[2], (MATERIALS,), jnp.float32, math.log(0.1), math.log(10.0))), 0.1, 10.0),
        "robin_table": jnp.clip(jnp.exp(jax.random.uniform(key_of[3], (ROBINS,), jnp.float32, math.log(0.5), math.log(8.0))), 0.5, 8.0),
        "robin_index": place_ends(jax.random.randint(key_of[4], (N_WIDE, N_NARROW, 2), 0, ROBINS), jax.random.fold_in(key_of[4], 1), 0, ROBINS - 1).astype(jnp.int32),
        "coarse_rows": scatter_about(key_of[5], (COARSE, COARSE), (COARSE * CX * CY * NZ) ** -0.5, 0.005859375, ((0, 32),), jnp.float32),
    }


reaction = 1.0


def spread_cells(blocks):
    size_a, size_b, size_c = blocks.shape
    grown_up = jnp.broadcast_to(blocks[:, None, :, None, :, None], (size_a, BLOCK, size_b, BLOCK, size_c, BLOCK))
    return grown_up.reshape(size_a * BLOCK, size_b * BLOCK, size_c * BLOCK)


def spread_face(blocks):
    size_a, size_b = blocks.shape
    grown_up = jnp.broadcast_to(blocks[:, None, :, None], (size_a, BLOCK, size_b, BLOCK))
    return grown_up.reshape(size_a * BLOCK, size_b * BLOCK)


def face_conduct(kappa, west_k, east_k, south_k, north_k):
    west_v = jnp.concatenate([west_k[None], kappa[:-1]], 0)
    east_v = jnp.concatenate([kappa[1:], east_k[None]], 0)
    south_v = jnp.concatenate([south_k[:, None], kappa[:, :-1]], 1)
    north_v = jnp.concatenate([kappa[:, 1:], north_k[:, None]], 1)
    below_v = jnp.concatenate([kappa[:, :, :1], kappa[:, :, :-1]], 2)
    above_v = jnp.concatenate([kappa[:, :, 1:], kappa[:, :, -1:]], 2)
    return (0.5 * (kappa + west_v), 0.5 * (kappa + east_v), 0.5 * (kappa + south_v),
            0.5 * (kappa + north_v), 0.5 * (kappa + below_v), 0.5 * (kappa + above_v))


def neighbour_sum(field_now, conduct, borders):
    zero_layer = jnp.zeros_like(field_now[:, :, :1])
    coupled = conduct[0] * jnp.concatenate([borders[0][None], field_now[:-1]], 0)
    coupled = coupled + conduct[1] * jnp.concatenate([field_now[1:], borders[1][None]], 0)
    coupled = coupled + conduct[2] * jnp.concatenate([borders[2][:, None], field_now[:, :-1]], 1)
    coupled = coupled + conduct[3] * jnp.concatenate([field_now[:, 1:], borders[3][:, None]], 1)
    coupled = coupled + conduct[4] * jnp.concatenate([zero_layer, field_now[:, :, :-1]], 2)
    return coupled + conduct[5] * jnp.concatenate([field_now[:, :, 1:], zero_layer], 2)


def side_marks(shape):
    index_x = lax.broadcasted_iota(jnp.int32, (shape[0], shape[1], 1), 0)
    index_y = lax.broadcasted_iota(jnp.int32, (shape[0], shape[1], 1), 1)
    return ((index_x == 0).astype(jnp.float32), (index_x == shape[0] - 1).astype(jnp.float32),
            (index_y == 0).astype(jnp.float32), (index_y == shape[1] - 1).astype(jnp.float32))


def assemble_local(material):
    kappa_blocks, west_b, east_b, south_b, north_b, inside, robin_pair = material
    kappa = spread_cells(kappa_blocks)
    sides = (spread_face(west_b), spread_face(east_b), spread_face(south_b), spread_face(north_b))
    owned = (kappa[0], kappa[-1], kappa[:, 0], kappa[:, -1])
    chosen = [jnp.where(inside[side] > 0, sides[side], owned[side]) for side in range(4)]
    conduct = face_conduct(kappa, chosen[0], chosen[1], chosen[2], chosen[3])
    conduct_sum = conduct[0] + conduct[1] + conduct[2] + conduct[3] + conduct[4] + conduct[5]
    marks = side_marks(kappa.shape)
    robin_term = robin_pair[0] * (inside[0] * marks[0] + inside[1] * marks[1]) + robin_pair[1] * (inside[2] * marks[2] + inside[3] * marks[3])
    parity = (lax.broadcasted_iota(jnp.int32, kappa.shape, 0) + lax.broadcasted_iota(jnp.int32, kappa.shape, 1)
              + lax.broadcasted_iota(jnp.int32, kappa.shape, 2)) % 2
    return conduct, conduct_sum, robin_term, parity


def robin_source(traces, shape):
    marks = side_marks(shape)
    return (marks[0] * traces[0][None] + marks[1] * traces[1][None]
            + marks[2] * traces[2][:, None] + marks[3] * traces[3][:, None])


def relax(field_now, source, conduct, diagonal, parity):
    blank_x = jnp.zeros_like(field_now[0])
    blank_y = jnp.zeros_like(field_now[:, 0])
    blanks = (blank_x, blank_x, blank_y, blank_y)
    for sweep_at in range(SWEEPS):
        for colour in range(2):
            update = (source + neighbour_sum(field_now, conduct, blanks)) / diagonal
            field_now = jnp.where(parity == colour, update, field_now)
    return field_now


def misfit(field_now, source_part, conduct, conduct_sum, borders):
    return source_part - (reaction + conduct_sum) * field_now + neighbour_sum(field_now, conduct, borders)


def coarse_weights(extent_x, extent_y):
    along_x = (jnp.arange(extent_x, dtype=jnp.float32) + 0.5) / extent_x
    along_y = (jnp.arange(extent_y, dtype=jnp.float32) + 0.5) / extent_y
    return ((1.0 - along_x)[:, None] * (1.0 - along_y)[None, :], along_x[:, None] * (1.0 - along_y)[None, :],
            (1.0 - along_x)[:, None] * along_y[None, :], along_x[:, None] * along_y[None, :])


def restrict(leftover):
    column_sum = jnp.sum(leftover, axis=2)
    weights = coarse_weights(leftover.shape[0], leftover.shape[1])
    return jnp.stack([jnp.sum(weights[corner] * column_sum) for corner in range(4)])


def interpolate(corners, extent_x, extent_y):
    weights = coarse_weights(extent_x, extent_y)
    return corners[0, 0] * weights[0] + corners[1, 0] * weights[1] + corners[0, 1] * weights[2] + corners[1, 1] * weights[3]


def robin_traces(field_now, borders, conduct, inside, robin_pair):
    return (inside[0] * (conduct[0][0] * borders[0] + robin_pair[0] * field_now[0]),
            inside[1] * (conduct[1][-1] * borders[1] + robin_pair[0] * field_now[-1]),
            inside[2] * (conduct[2][:, 0] * borders[2] + robin_pair[1] * field_now[:, 0]),
            inside[3] * (conduct[3][:, -1] * borders[3] + robin_pair[1] * field_now[:, -1]))


def combine_partials(stacked):
    from_west = jnp.pad(stacked[:-1, :, 1], ((1, 0), (0, 0)))
    from_south = jnp.pad(stacked[:, :-1, 2], ((0, 0), (1, 0)))
    from_corner = jnp.pad(stacked[:-1, :-1, 3], ((1, 0), (1, 0)))
    return stacked[:, :, 0] + from_west + from_south + from_corner


def reference(right_side, labels, material_table, robin_table, robin_index, coarse_rows):
    blocks_total = N_WIDE * N_NARROW
    blocks_x, blocks_y, blocks_z = CX // BLOCK, CY // BLOCK, NZ // BLOCK

    def flat_blocks(array):
        return array.reshape((blocks_total,) + array.shape[2:])

    kappa_blocks = material_table[labels].reshape(N_WIDE, blocks_x, N_NARROW, blocks_y, blocks_z).transpose(0, 2, 1, 3, 4)
    west_b = jnp.concatenate([kappa_blocks[:1, :, 0], kappa_blocks[:-1, :, -1]], 0)
    east_b = jnp.concatenate([kappa_blocks[1:, :, 0], kappa_blocks[-1:, :, -1]], 0)
    south_b = jnp.concatenate([kappa_blocks[:, :1, :, 0], kappa_blocks[:, :-1, :, -1]], 1)
    north_b = jnp.concatenate([kappa_blocks[:, 1:, :, 0], kappa_blocks[:, -1:, :, -1]], 1)
    wide_pos = jnp.arange(N_WIDE)[:, None] + jnp.zeros((1, N_NARROW), jnp.int32)
    narrow_pos = jnp.arange(N_NARROW)[None, :] + jnp.zeros((N_WIDE, 1), jnp.int32)
    inside = jnp.stack([wide_pos > 0, wide_pos < N_WIDE - 1, narrow_pos > 0, narrow_pos < N_NARROW - 1], -1).astype(jnp.float32)
    robin_pair = robin_table[robin_index]
    material = tuple(flat_blocks(item) for item in (kappa_blocks, west_b, east_b, south_b, north_b, inside, robin_pair))
    source_blocks = flat_blocks(right_side.reshape(N_WIDE, CX, N_NARROW, CY, NZ).transpose(0, 2, 1, 3, 4))

    def outer_borders(solution_now):
        stacked = solution_now.reshape(N_WIDE, N_NARROW, CX, CY, NZ)
        zero_x = jnp.zeros_like(stacked[:1, :, 0])
        zero_y = jnp.zeros_like(stacked[:, :1, :, 0])
        west_f = jnp.concatenate([zero_x, stacked[:-1, :, -1]], 0)
        east_f = jnp.concatenate([stacked[1:, :, 0], zero_x], 0)
        south_f = jnp.concatenate([zero_y, stacked[:, :-1, :, -1]], 1)
        north_f = jnp.concatenate([stacked[:, 1:, :, 0], zero_y], 1)
        return tuple(flat_blocks(item) for item in (west_f, east_f, south_f, north_f))

    def sweep_block(packed):
        field_now, source_part, traces, local_mat = packed
        conduct, conduct_sum, robin_term, parity = assemble_local(local_mat)
        source = source_part + robin_source(traces, field_now.shape)
        diagonal = reaction + conduct_sum + robin_term
        return relax(field_now, source, conduct, diagonal, parity)

    def partial_block(packed):
        field_now, source_part, borders, local_mat = packed
        conduct, conduct_sum, robin_term, parity = assemble_local(local_mat)
        return restrict(misfit(field_now, source_part, conduct, conduct_sum, borders))

    def correct_block(packed):
        field_now, window = packed
        return field_now + interpolate(window[1:3, 1:3], CX, CY)[:, :, None]

    def trace_block(packed):
        field_now, borders, local_mat = packed
        conduct, conduct_sum, robin_term, parity = assemble_local(local_mat)
        return robin_traces(field_now, borders, conduct, local_mat[5], local_mat[6])

    def final_block(packed):
        field_now, source_part, borders, local_mat = packed
        conduct, conduct_sum, robin_term, parity = assemble_local(local_mat)
        return misfit(field_now, source_part, conduct, conduct_sum, borders)

    solution_now = jnp.zeros((blocks_total, CX, CY, NZ), jnp.float32)
    traces = (jnp.zeros((blocks_total, CY, NZ), jnp.float32), jnp.zeros((blocks_total, CY, NZ), jnp.float32),
              jnp.zeros((blocks_total, CX, NZ), jnp.float32), jnp.zeros((blocks_total, CX, NZ), jnp.float32))
    for outer in range(ITERS):
        solution_now = lax.map(sweep_block, (solution_now, source_blocks, traces, material))
        borders = outer_borders(solution_now)
        partials = lax.map(partial_block, (solution_now, source_blocks, borders, material))
        coarse_vec = combine_partials(partials.reshape(N_WIDE, N_NARROW, 4)).reshape(-1)
        coarse_all = jnp.dot(coarse_rows, coarse_vec, precision=lax.Precision.HIGHEST, preferred_element_type=jnp.float32)
        coarse_grid = jnp.pad(coarse_all.reshape(N_WIDE, N_NARROW), ((1, 2), (1, 2)))
        window_rows = [jnp.stack([coarse_grid[offset_x:offset_x + N_WIDE, offset_y:offset_y + N_NARROW] for offset_y in range(4)], -1)
                       for offset_x in range(4)]
        windows = flat_blocks(jnp.stack(window_rows, -2))
        solution_now = lax.map(correct_block, (solution_now, windows))
        borders = outer_borders(solution_now)
        if outer + 1 < ITERS:
            traces = lax.map(trace_block, (solution_now, borders, material))
    leftover = lax.map(final_block, (solution_now, source_blocks, borders, material))

    def to_grid(blocks):
        return blocks.reshape(N_WIDE, N_NARROW, CX, CY, NZ).transpose(0, 2, 1, 3, 4).reshape(NX, NY, NZ)

    return to_grid(solution_now).astype(jnp.bfloat16), to_grid(leftover).astype(jnp.bfloat16)
```

```python
import jax
import jax.numpy as jnp
from jax import lax
from jax.experimental import pallas as pl
from jax.experimental.pallas import tpu as pltpu
from jax.sharding import PartitionSpec as P

BLOCK = 8
SWEEPS = 4
ITERS = 2
reaction = 1.0
MESH = pl.DeviceIdType.MESH
SIDES = ((-1, 0), (1, 0), (0, -1), (0, 1))
SLOTS = [(a, b) for a in range(-1, 3) for b in range(-1, 3) if a in (0, 1) or b in (0, 1)]


def slot_at(a, b):
    return 4 * (a + 1) + (b + 1)


def make_kernel(wide, narrow, shape, blocks):
    cx, cy, nz = shape
    half = cx // 2
    count = wide * narrow
    blocks_x, blocks_y, blocks_z = blocks
    f32 = jnp.float32

    def kernel(
        rhs_hbm, labels_hbm, material, robin_table, robin_index, rows_hbm,
        sol_ref, res_ref,
        rhs, labels, labels_in, window, gathered, x_out, x_in, y_out, y_in, coef, diag_s,
        local_sem, label_send, label_recv, row_send, row_recv,
        face_send, face_recv, gather_send, gather_recv,
    ):
        w = lax.axis_index("wide")
        n = lax.axis_index("narrow")
        me = w * narrow + n
        loads = [
            pltpu.make_async_copy(labels_hbm, labels, local_sem.at[0]),
            pltpu.make_async_copy(rows_hbm, window.at[slot_at(0, 0)], local_sem.at[1]),
            pltpu.make_async_copy(rhs_hbm, rhs, local_sem.at[2]),
        ]
        labels_in[...] = jnp.zeros_like(labels_in)
        x_in[...] = jnp.zeros_like(x_in)
        y_in[...] = jnp.zeros_like(y_in)
        for a, b in SLOTS:
            if (a, b) != (0, 0):
                window[slot_at(a, b)] = jnp.zeros_like(window[slot_at(a, b)])
        for load in loads:
            load.start()
        barrier = pltpu.get_barrier_semaphore()

        def peer(step):
            flat = me + step
            flat = jnp.where(flat >= count, flat - count, flat)
            return (flat // narrow, flat % narrow)

        def greet(step, carry):
            pl.semaphore_signal(barrier, inc=1, device_id=peer(step), device_id_type=MESH)
            return carry

        lax.fori_loop(1, count, greet, 0)

        has = [w > 0, w < wide - 1, n > 0, n < narrow - 1]
        inside = [jnp.where(flag, 1.0, 0.0).astype(f32) for flag in has]
        p_x = robin_table[robin_index[0, 0, 0]]
        p_y = robin_table[robin_index[0, 0, 1]]

        spread = (
            lax.broadcasted_iota(jnp.int32, (blocks_z, nz), 1) // BLOCK
            == lax.broadcasted_iota(jnp.int32, (blocks_z, nz), 0)
        ).astype(f32)
        row_j = lax.broadcasted_iota(jnp.int32, (cy, nz), 0)
        lane_k = lax.broadcasted_iota(jnp.int32, (cy, nz), 1)
        even = (row_j + lane_k) % 2 == 0

        def kappa_rows(label_rows):
            wide_rows = jnp.dot(label_rows.astype(f32), spread, preferred_element_type=f32)
            found = jnp.zeros_like(wide_rows)
            for entry in range(material.shape[0]):
                found = jnp.where(wide_rows == float(entry), material[entry], found)
            return found

        def plane_of(rows):
            plane = jnp.broadcast_to(rows[blocks_y - 1 : blocks_y], (cy, nz))
            for at in range(blocks_y - 2, -1, -1):
                plane = jnp.where(row_j < (at + 1) * BLOCK, jnp.broadcast_to(rows[at : at + 1], (cy, nz)), plane)
            return plane

        loads[0].wait()
        loads[1].wait()
        kappa = [plane_of(kappa_rows(labels[bx])) for bx in range(blocks_x)]
        c_below, c_above = [], []
        for plane in kappa:
            c_below.append(0.5 * (plane + jnp.where(lane_k == 0, plane, pltpu.roll(plane, 1, 1))))
            c_above.append(0.5 * (plane + jnp.where(lane_k == nz - 1, plane, pltpu.roll(plane, nz - 1, 1))))

        pl.semaphore_wait(barrier, count - 1)

        def label_copy(side):
            dw, dn = SIDES[side]
            return pltpu.make_async_remote_copy(
                src_ref=labels, dst_ref=labels_in.at[side ^ 1],
                send_sem=label_send.at[side], recv_sem=label_recv.at[side ^ 1],
                device_id=(w + dw, n + dn), device_id_type=MESH,
            )

        def label_arrival(side):
            dw, dn = SIDES[side]
            return pltpu.make_async_remote_copy(
                src_ref=labels, dst_ref=labels_in.at[side],
                send_sem=label_send.at[side], recv_sem=label_recv.at[side],
                device_id=(w + dw, n + dn), device_id_type=MESH,
            )

        for side in range(4):
            @pl.when(has[side])
            def _(side=side):
                label_copy(side).start()

        def on_grid(a, b):
            return (w + a >= 0) & (w + a < wide) & (n + b >= 0) & (n + b < narrow)

        def row_copy(a, b):
            slot = slot_at(a, b)
            return pltpu.make_async_remote_copy(
                src_ref=window.at[slot_at(0, 0)], dst_ref=window.at[slot],
                send_sem=row_send.at[slot], recv_sem=row_recv.at[slot],
                device_id=(w - a, n - b), device_id_type=MESH,
            )

        far = [(a, b) for a, b in SLOTS if (a, b) != (0, 0) and abs(a) < wide and abs(b) < narrow]
        for a, b in far:
            @pl.when(on_grid(-a, -b))
            def _(a=a, b=b):
                row_copy(a, b).start()

        loads[2].wait()
        for side in range(4):
            @pl.when(has[side])
            def _(side=side):
                label_arrival(side).wait_recv()

        west_k = jnp.where(has[0], plane_of(kappa_rows(labels_in[0, blocks_x - 1])), kappa[0])
        east_k = jnp.where(has[1], plane_of(kappa_rows(labels_in[1, 0])), kappa[-1])
        c_south, c_north = [], []
        for bx in range(blocks_x):
            plane = kappa[bx]
            south_row = jnp.broadcast_to(kappa_rows(labels_in[2, bx])[blocks_y - 1 : blocks_y], (cy, nz))
            north_row = jnp.broadcast_to(kappa_rows(labels_in[3, bx])[0:1], (cy, nz))
            below = jnp.where(has[2], south_row, plane)
            above = jnp.where(has[3], north_row, plane)
            c_south.append(0.5 * (plane + jnp.where(row_j == 0, below, pltpu.roll(plane, 1, 0))))
            c_north.append(0.5 * (plane + jnp.where(row_j == cy - 1, above, pltpu.roll(plane, cy - 1, 0))))

        def x_face(i):
            left = west_k if i == 0 else kappa[(i - 1) // BLOCK]
            right = east_k if i == cx else kappa[i // BLOCK]
            return left if left is right else 0.5 * (left + right)

        faces = {}
        for i in range(cx + 1):
            key = (min(max(i - 1, -1), cx) // BLOCK, i // BLOCK)
            if key not in faces:
                faces[key] = x_face(i)
        c_x = [faces[((i - 1) // BLOCK if i else -1, i // BLOCK)] for i in range(cx + 1)]

        zero = jnp.zeros((cy, nz), f32)
        loc_south = [jnp.where(row_j == 0, 0.0, c) for c in c_south]
        loc_north = [jnp.where(row_j == cy - 1, 0.0, c) for c in c_north]
        loc_below = [jnp.where(lane_k == 0, 0.0, c) for c in c_below]
        loc_above = [jnp.where(lane_k == nz - 1, 0.0, c) for c in c_above]
        rob_y = p_y * (inside[2] * (row_j == 0).astype(f32) + inside[3] * (row_j == cy - 1).astype(f32))
        known = {}

        def plane_terms(i):
            bx = i // BLOCK
            key = (bx, i % BLOCK == 0, i % BLOCK == BLOCK - 1)
            if key not in known:
                total = reaction + c_x[i] + c_x[i + 1] + c_south[bx] + c_north[bx] + c_below[bx] + c_above[bx]
                local = total + rob_y
                if i == 0:
                    local = local + p_x * inside[0]
                if i == cx - 1:
                    local = local + p_x * inside[1]
                inv = 1.0 / local
                west = zero if i == 0 else c_x[i] * inv
                east = zero if i == cx - 1 else c_x[i + 1] * inv
                known[key] = (
                    total, inv, west, east, loc_south[bx] * inv, loc_north[bx] * inv,
                    loc_below[bx] * inv, loc_above[bx] * inv,
                )
            return known[key]

        for h in range(half):
            lo, hi = plane_terms(2 * h), plane_terms(2 * h + 1)
            diag_s[0, h] = lo[0]
            diag_s[1, h] = hi[0]
            for colour in range(2):
                low = even if colour == 0 else jnp.logical_not(even)
                coef[colour, 0, h] = jnp.where(low, lo[3], hi[2])
                coef[colour, 1, h] = jnp.where(low, lo[2], hi[3])
                for item in range(4):
                    coef[colour, 2 + item, h] = jnp.where(low, lo[4 + item], hi[4 + item])
                coef[colour, 6, h] = jnp.where(low, lo[1], hi[1])

        def stacked(planes):
            return jnp.stack(planes, 0)

        def by_block(planes, parity):
            return stacked([planes[(2 * h + parity) // BLOCK] for h in range(half)])

        even3 = jnp.broadcast_to(even[None], (half, cy, nz))

        def packed(pair):
            return jnp.where(even3, pair[0], pair[1]), jnp.where(even3, pair[1], pair[0])

        def up(v):
            return jnp.concatenate([v[1:], v[:1]], 0)

        def down(v):
            return jnp.concatenate([v[-1:], v[:-1]], 0)

        def coupling(other, colour):
            if colour == 0:
                across = jnp.where(even3, down(other), up(other))
            else:
                across = jnp.where(even3, up(other), down(other))
            total = coef[colour, 0] * other + coef[colour, 1] * across
            total = total + coef[colour, 2] * pltpu.roll(other, 1, 1)
            total = total + coef[colour, 3] * pltpu.roll(other, cy - 1, 1)
            total = total + coef[colour, 4] * pltpu.roll(other, 1, 2)
            return total + coef[colour, 5] * pltpu.roll(other, nz - 1, 2)

        def relax(red, black, source):
            scaled = packed(source)
            scaled = (scaled[0] * coef[0, 6], scaled[1] * coef[1, 6])
            for sweep in range(SWEEPS):
                red = scaled[0] if black is None else scaled[0] + coupling(black, 0)
                black = scaled[1] + coupling(red, 1)
            return red, black

        right = tuple(stacked([rhs[2 * h + parity] for h in range(half)]) for parity in range(2))

        def misfit(u):
            result = []
            for parity in range(2):
                mine, other = u[parity], u[1 - parity]
                faces_w = stacked([zero if 2 * h + parity == 0 else c_x[2 * h + parity] for h in range(half)])
                faces_e = stacked(
                    [zero if 2 * h + parity == cx - 1 else c_x[2 * h + parity + 1] for h in range(half)]
                )
                west = down(other) if parity == 0 else other
                east = other if parity == 0 else up(other)
                total = right[parity] - diag_s[parity] * mine + faces_w * west + faces_e * east
                total = total + by_block(loc_south, parity) * pltpu.roll(mine, 1, 1)
                total = total + by_block(loc_north, parity) * pltpu.roll(mine, cy - 1, 1)
                total = total + by_block(loc_below, parity) * pltpu.roll(mine, 1, 2)
                total = total + by_block(loc_above, parity) * pltpu.roll(mine, nz - 1, 2)
                result.append(total)
            return result

        xi = [(i + 0.5) / cx for i in range(cx)]
        eta = (row_j.astype(f32) + 0.5) / cy
        eta_first, eta_last = 0.5 / cy, (cy - 0.5) / cy

        def weigh_x(pair):
            lows, highs = None, None
            for i in range(cx):
                plane = pair[i % 2][i // 2]
                low, high = (1.0 - xi[i]) * plane, xi[i] * plane
                lows = low if lows is None else lows + low
                highs = high if highs is None else highs + high
            return lows, highs

        win_row = lax.broadcasted_iota(jnp.int32, (16, count), 0)
        win_lane = lax.broadcasted_iota(jnp.int32, (16, count), 1)
        point_w = w + win_row // 4 - 1
        point_n = n + win_row % 4 - 1
        point_ok = (point_w >= 0) & (point_w < wide) & (point_n >= 0) & (point_n < narrow)
        point = jnp.where(point_ok, point_w * narrow + point_n, -1)
        at_point = point == win_lane
        slot_row = lax.broadcasted_iota(jnp.int32, (16, nz), 0)

        def edge_coef(planes, parity, row):
            return stacked([planes[(2 * h + parity) // BLOCK][row : row + 1] for h in range(half)])

        south_c = [edge_coef(c_south, parity, 0) * inside[2] for parity in range(2)]
        north_c = [edge_coef(c_north, parity, cy - 1) * inside[3] for parity in range(2)]
        west_c = c_x[0] * inside[0]
        east_c = c_x[cx] * inside[1]

        def restrict(u):
            low, high = weigh_x(misfit(u))
            out_w = west_c * u[0][0]
            out_e = east_c * u[1][half - 1]
            sums = {
                -1: (1.0 - xi[-1]) * out_w,
                0: low + xi[-1] * out_w,
                1: high + (1.0 - xi[0]) * out_e,
                2: xi[0] * out_e,
            }
            out_s = weigh_x([south_c[parity] * u[parity][:, 0:1] for parity in range(2)])
            out_n = weigh_x([north_c[parity] * u[parity][:, cy - 1 : cy] for parity in range(2)])
            table = jnp.zeros((16, nz), f32)
            for a in range(-1, 3):
                near = jnp.sum(sums[a] * (1.0 - eta), 0, keepdims=True)
                away = jnp.sum(sums[a] * eta, 0, keepdims=True)
                entries = {0: near, 1: away}
                if a in (0, 1):
                    entries[-1] = (1.0 - eta_last) * out_s[a]
                    entries[0] = near + eta_last * out_s[a]
                    entries[1] = away + (1.0 - eta_first) * out_n[a]
                    entries[2] = eta_first * out_n[a]
                for b, entry in entries.items():
                    table = jnp.where(slot_row == slot_at(a, b), jnp.broadcast_to(entry, (16, nz)), table)
            summed = jnp.sum(table, 1, keepdims=True)
            return jnp.sum(jnp.where(at_point, summed, 0.0), 0, keepdims=True)

        def face_copy(turn, side):
            dw, dn = SIDES[side]
            if side < 2:
                source, target = x_out.at[turn, side], x_in.at[turn, side ^ 1]
            else:
                source, target = y_out.at[turn, side - 2], y_in.at[turn, (side ^ 1) - 2]
            return pltpu.make_async_remote_copy(
                src_ref=source, dst_ref=target,
                send_sem=face_send.at[turn, side], recv_sem=face_recv.at[turn, side ^ 1],
                device_id=(w + dw, n + dn), device_id_type=MESH,
            )

        def face_arrival(turn, side):
            dw, dn = SIDES[side]
            if side < 2:
                source, target = x_out.at[turn, side], x_in.at[turn, side]
            else:
                source, target = y_out.at[turn, side - 2], y_in.at[turn, side - 2]
            return pltpu.make_async_remote_copy(
                src_ref=source, dst_ref=target,
                send_sem=face_send.at[turn, side], recv_sem=face_recv.at[turn, side],
                device_id=(w + dw, n + dn), device_id_type=MESH,
            )

        def gather_all(turn):
            return pltpu.make_async_remote_copy(
                src_ref=gathered.at[turn, pl.ds(0, count - 1)], dst_ref=gathered.at[turn, pl.ds(0, count - 1)],
                send_sem=gather_send.at[turn], recv_sem=gather_recv.at[turn],
                device_id=peer(1), device_id_type=MESH,
            )

        red = black = None
        source = right
        for turn in range(ITERS):
            red, black = relax(red, black, source)
            u = [jnp.where(even3, red, black), jnp.where(even3, black, red)]
            x_out[turn, 0] = u[0][0]
            x_out[turn, 1] = u[1][half - 1]
            for parity in range(2):
                y_out[turn, 0, pl.ds(parity * half, half)] = u[parity][:, 0:1]
                y_out[turn, 1, pl.ds(parity * half, half)] = u[parity][:, cy - 1 : cy]
            for side in range(4):
                @pl.when(has[side])
                def _(turn=turn, side=side):
                    face_copy(turn, side).start()
            gathered[turn, me] = restrict(u)

            def scatter(step, carry, turn=turn):
                pltpu.make_async_remote_copy(
                    src_ref=gathered.at[turn, me], dst_ref=gathered.at[turn, me],
                    send_sem=gather_send.at[turn], recv_sem=gather_recv.at[turn],
                    device_id=peer(step), device_id_type=MESH,
                ).start()
                return carry

            lax.fori_loop(1, count, scatter, 0)
            for side in range(4):
                @pl.when(has[side])
                def _(turn=turn, side=side):
                    face_arrival(turn, side).wait_recv()
            if turn == 0:
                for a, b in far:
                    @pl.when(on_grid(a, b))
                    def _(a=a, b=b):
                        row_copy(a, b).wait_recv()
            gather_all(turn).wait_recv()
            load = jnp.sum(gathered[turn], 0)
            value = {}
            for a, b in SLOTS:
                value[a, b] = jnp.sum(window[slot_at(a, b)] * load, 1, keepdims=True)

            along = {a: value[a, 0] * (1.0 - eta) + value[a, 1] * eta for a in range(-1, 3)}
            u = [
                u[parity]
                + stacked(
                    [
                        (1.0 - xi[2 * h + parity]) * along[0] + xi[2 * h + parity] * along[1]
                        for h in range(half)
                    ]
                )
                for parity in range(2)
            ]
            west_u = x_in[turn, 0] + (1.0 - xi[-1]) * along[-1] + xi[-1] * along[0]
            east_u = x_in[turn, 1] + (1.0 - xi[0]) * along[1] + xi[0] * along[2]
            under = [value[a, -1] * (1.0 - eta_last) + value[a, 0] * eta_last for a in (0, 1)]
            over = [value[a, 1] * (1.0 - eta_first) + value[a, 2] * eta_first for a in (0, 1)]

            def edge(base, ends, parity):
                return base + stacked(
                    [
                        jnp.broadcast_to(
                            (1.0 - xi[2 * h + parity]) * ends[0] + xi[2 * h + parity] * ends[1], (1, nz)
                        )
                        for h in range(half)
                    ]
                )

            south_u = [edge(y_in[turn, 0, pl.ds(parity * half, half)], under, parity) for parity in range(2)]
            north_u = [edge(y_in[turn, 1, pl.ds(parity * half, half)], over, parity) for parity in range(2)]
            out_x = [west_c * west_u, east_c * east_u]
            out_y = [[south_c[parity] * south_u[parity] for parity in range(2)],
                     [north_c[parity] * north_u[parity] for parity in range(2)]]
            last = turn + 1 == ITERS
            if not last:
                out_x[0] = out_x[0] + (inside[0] * p_x) * u[0][0]
                out_x[1] = out_x[1] + (inside[1] * p_x) * u[1][half - 1]
                for parity in range(2):
                    out_y[0][parity] = out_y[0][parity] + (inside[2] * p_y) * u[parity][:, 0:1]
                    out_y[1][parity] = out_y[1][parity] + (inside[3] * p_y) * u[parity][:, cy - 1 : cy]
            base = misfit(u) if last else right
            row3 = jnp.broadcast_to(row_j[None], (half, cy, nz))
            total = []
            for parity in range(2):
                ends = jnp.where(row3 == 0, jnp.broadcast_to(out_y[0][parity], row3.shape), 0.0)
                ends = jnp.where(row3 == cy - 1, jnp.broadcast_to(out_y[1][parity], row3.shape), ends)
                total.append(base[parity] + ends)
            total[0] = jnp.concatenate([total[0][:1] + out_x[0][None], total[0][1:]], 0)
            total[1] = jnp.concatenate([total[1][:-1], total[1][-1:] + out_x[1][None]], 0)
            if last:
                for i in range(cx):
                    sol_ref[i] = u[i % 2][i // 2].astype(jnp.bfloat16)
                    res_ref[i] = total[i % 2][i // 2].astype(jnp.bfloat16)
            else:
                source = total
                red, black = packed(u)

        for side in range(4):
            @pl.when(has[side])
            def _(side=side):
                label_copy(side).wait_send()
                for turn in range(ITERS):
                    face_copy(turn, side).wait_send()
        for a, b in far:
            @pl.when(on_grid(-a, -b))
            def _(a=a, b=b):
                row_copy(a, b).wait_send()
        for turn in range(ITERS):
            gather_all(turn).wait_send()

    scratch = [
        pltpu.VMEM(shape, f32),
        pltpu.VMEM(blocks, jnp.int32),
        pltpu.VMEM((4,) + blocks, jnp.int32),
        pltpu.VMEM((16, 1, count), f32),
        pltpu.VMEM((ITERS, count, 1, count), f32),
        pltpu.VMEM((ITERS, 2, cy, nz), f32),
        pltpu.VMEM((ITERS, 2, cy, nz), f32),
        pltpu.VMEM((ITERS, 2, cx, 1, nz), f32),
        pltpu.VMEM((ITERS, 2, cx, 1, nz), f32),
        pltpu.VMEM((2, 7, half, cy, nz), f32),
        pltpu.VMEM((2, half, cy, nz), f32),
        pltpu.SemaphoreType.DMA((3,)),
        pltpu.SemaphoreType.DMA((4,)),
        pltpu.SemaphoreType.DMA((4,)),
        pltpu.SemaphoreType.DMA((16,)),
        pltpu.SemaphoreType.DMA((16,)),
        pltpu.SemaphoreType.DMA((ITERS, 4)),
        pltpu.SemaphoreType.DMA((ITERS, 4)),
        pltpu.SemaphoreType.DMA((ITERS,)),
        pltpu.SemaphoreType.DMA((ITERS,)),
    ]
    return kernel, scratch


def solution(mesh):
    wide, narrow = mesh.shape["wide"], mesh.shape["narrow"]

    def body(right_side, labels, material_table, robin_table, robin_index, coarse_rows):
        shape = right_side.shape
        kernel, scratch = make_kernel(wide, narrow, shape, labels.shape)
        anywhere = pl.BlockSpec(memory_space=pl.ANY)
        scalars = pl.BlockSpec(memory_space=pltpu.SMEM)
        vectors = pl.BlockSpec(memory_space=pltpu.VMEM)
        return pl.pallas_call(
            kernel,
            out_shape=(jax.ShapeDtypeStruct(shape, jnp.bfloat16),) * 2,
            in_specs=[anywhere, anywhere, scalars, scalars, scalars, anywhere],
            out_specs=(vectors, vectors),
            scratch_shapes=scratch,
            compiler_params=pltpu.CompilerParams(collective_id=0, has_side_effects=True),
        )(right_side, labels, material_table, robin_table, robin_index, coarse_rows)

    cells = P("wide", "narrow", None)
    return jax.shard_map(
        body,
        mesh=mesh,
        in_specs=(cells, cells, P(), P(), cells, P(("wide", "narrow"), None)),
        out_specs=(cells, cells),
        check_vma=False,
    )
```

```python
import jax
import jax.numpy as jnp
from jax import lax
from jax.experimental import pallas as pl
from jax.experimental.pallas import tpu as pltpu
from jax.sharding import PartitionSpec as P

BLOCK = 8
SWEEPS = 4
ITERS = 2
reaction = 1.0
MESH = pl.DeviceIdType.MESH
SIDES = ((-1, 0), (1, 0), (0, -1), (0, 1))
SLOTS = [(a, b) for a in range(-1, 3) for b in range(-1, 3) if a in (0, 1) or b in (0, 1)]


def slot_at(a, b):
    return 4 * (a + 1) + (b + 1)


def make_kernel(wide, narrow, shape, blocks):
    cx, cy, nz = shape
    half = cx // 2
    count = wide * narrow
    low = 1
    while low * low < wide or wide % low:
        low += 1
    high = wide // low
    group = low * narrow
    blocks_x, blocks_y, blocks_z = blocks
    f32 = jnp.float32

    def kernel(
        rhs_hbm, labels_hbm, material, robin_table, robin_index, rows_hbm,
        sol_ref, res_ref,
        rhs, labels, labels_in, window, near_sums, far_sums, x_out, x_in, y_out, y_in, coef, diag_s,
        local_sem, label_send, label_recv, row_send, row_recv,
        face_send, face_recv, near_send, near_recv, far_send, far_recv,
    ):
        w = lax.axis_index("wide")
        n = lax.axis_index("narrow")
        loads = [
            pltpu.make_async_copy(labels_hbm, labels, local_sem.at[0]),
            pltpu.make_async_copy(rows_hbm, window.at[slot_at(0, 0)], local_sem.at[1]),
            pltpu.make_async_copy(rhs_hbm, rhs, local_sem.at[2]),
        ]
        labels_in[...] = jnp.zeros_like(labels_in)
        x_in[...] = jnp.zeros_like(x_in)
        y_in[...] = jnp.zeros_like(y_in)
        for slot in range(16):
            if slot != slot_at(0, 0):
                window[slot] = jnp.zeros_like(window[slot])
        for load in loads:
            load.start()
        barrier = pltpu.get_barrier_semaphore()

        w_low, w_high = w % low, w // low

        def near_peer(dw, dn):
            return (w_high * low + (w_low + dw) % low, (n + dn) % narrow)

        def far_peer(dw):
            return ((w_high + dw) % high * low + w_low, n)

        near = [(dw, dn) for dw in range(low) for dn in range(narrow)][:0:-1]
        afar = list(range(1, high))
        over_west = (w_low == 0) & (w > 0)
        over_east = (w_low == low - 1) & (w < wide - 1)

        def greet(target):
            pl.semaphore_signal(barrier, inc=1, device_id=target, device_id_type=MESH)

        @pl.when(over_west)
        def _():
            greet((w - 1, n))

        @pl.when(over_east)
        def _():
            greet((w + 1, n))

        for dw in afar:
            greet(far_peer(dw))
        for dw, dn in near:
            greet(near_peer(dw, dn))

        has = [w > 0, w < wide - 1, n > 0, n < narrow - 1]
        inside = [jnp.where(flag, 1.0, 0.0).astype(f32) for flag in has]
        p_x = robin_table[robin_index[0, 0, 0]]
        p_y = robin_table[robin_index[0, 0, 1]]

        spread = (
            lax.broadcasted_iota(jnp.int32, (blocks_z, nz), 1) // BLOCK
            == lax.broadcasted_iota(jnp.int32, (blocks_z, nz), 0)
        ).astype(f32)
        row_j = lax.broadcasted_iota(jnp.int32, (cy, nz), 0)
        lane_k = lax.broadcasted_iota(jnp.int32, (cy, nz), 1)
        even = (row_j + lane_k) % 2 == 0

        def kappa_rows(label_rows):
            wide_rows = jnp.dot(label_rows.astype(f32), spread, preferred_element_type=f32)
            found = jnp.zeros_like(wide_rows)
            for entry in range(material.shape[0]):
                found = jnp.where(wide_rows == float(entry), material[entry], found)
            return found

        def plane_of(rows):
            plane = jnp.broadcast_to(rows[blocks_y - 1 : blocks_y], (cy, nz))
            for at in range(blocks_y - 2, -1, -1):
                plane = jnp.where(row_j < (at + 1) * BLOCK, jnp.broadcast_to(rows[at : at + 1], (cy, nz)), plane)
            return plane

        loads[0].wait()
        loads[1].wait()
        kappa = [plane_of(kappa_rows(labels[bx])) for bx in range(blocks_x)]
        c_below, c_above = [], []
        for plane in kappa:
            c_below.append(0.5 * (plane + jnp.where(lane_k == 0, plane, pltpu.roll(plane, 1, 1))))
            c_above.append(0.5 * (plane + jnp.where(lane_k == nz - 1, plane, pltpu.roll(plane, nz - 1, 1))))

        greeted = group + high - 2
        pl.semaphore_wait(barrier, greeted + jnp.where(over_west, 1, 0) + jnp.where(over_east, 1, 0))

        def label_copy(side):
            dw, dn = SIDES[side]
            return pltpu.make_async_remote_copy(
                src_ref=labels, dst_ref=labels_in.at[side ^ 1],
                send_sem=label_send.at[side], recv_sem=label_recv.at[side ^ 1],
                device_id=(w + dw, n + dn), device_id_type=MESH,
            )

        def label_arrival(side):
            dw, dn = SIDES[side]
            return pltpu.make_async_remote_copy(
                src_ref=labels, dst_ref=labels_in.at[side],
                send_sem=label_send.at[side], recv_sem=label_recv.at[side],
                device_id=(w + dw, n + dn), device_id_type=MESH,
            )

        for side in range(4):
            @pl.when(has[side])
            def _(side=side):
                label_copy(side).start()

        def row_step(kind, at, source, target, dw, dn):
            return pltpu.make_async_remote_copy(
                src_ref=source, dst_ref=target, send_sem=row_send.at[kind, at], recv_sem=row_recv.at[kind, at],
                device_id=(w + dw, n + dn), device_id_type=MESH,
            )

        def column(a):
            return window.at[pl.ds(4 * (a + 1), 4)]

        own_row = window.at[slot_at(0, 0)]
        row_south = row_step(0, 0, own_row, window.at[slot_at(0, 1)], 0, -1)
        row_north = row_step(0, 1, own_row, window.at[slot_at(0, -1)], 0, 1)
        row_again = row_step(1, 0, window.at[slot_at(0, 1)], window.at[slot_at(0, 2)], 0, -1)
        column_west = row_step(2, 0, column(0), column(1), -1, 0)
        column_east = row_step(2, 1, column(0), column(-1), 1, 0)
        column_again = row_step(3, 0, column(1), column(2), -1, 0)
        pl.when(has[2])(row_south.start)
        pl.when(has[3])(row_north.start)

        for side in (2, 3):
            @pl.when(has[side])
            def _(side=side):
                label_arrival(side).wait_recv()

        c_south, c_north = [], []
        for bx in range(blocks_x):
            plane = kappa[bx]
            south_row = jnp.broadcast_to(kappa_rows(labels_in[2, bx])[blocks_y - 1 : blocks_y], (cy, nz))
            north_row = jnp.broadcast_to(kappa_rows(labels_in[3, bx])[0:1], (cy, nz))
            below = jnp.where(has[2], south_row, plane)
            above = jnp.where(has[3], north_row, plane)
            c_south.append(0.5 * (plane + jnp.where(row_j == 0, below, pltpu.roll(plane, 1, 0))))
            c_north.append(0.5 * (plane + jnp.where(row_j == cy - 1, above, pltpu.roll(plane, cy - 1, 0))))

        between = [0.5 * (kappa[bx] + kappa[bx + 1]) for bx in range(blocks_x - 1)]
        c_x = [
            kappa[i // BLOCK] if i % BLOCK else between[i // BLOCK - 1] if 0 < i < cx else None
            for i in range(cx + 1)
        ]

        zero = jnp.zeros((cy, nz), f32)
        loc_south = [jnp.where(row_j == 0, 0.0, c) for c in c_south]
        loc_north = [jnp.where(row_j == cy - 1, 0.0, c) for c in c_north]
        loc_below = [jnp.where(lane_k == 0, 0.0, c) for c in c_below]
        loc_above = [jnp.where(lane_k == nz - 1, 0.0, c) for c in c_above]
        rob_y = p_y * (inside[2] * (row_j == 0).astype(f32) + inside[3] * (row_j == cy - 1).astype(f32))
        known = {}

        def plane_terms(i):
            bx = i // BLOCK
            key = (bx, i % BLOCK == 0, i % BLOCK == BLOCK - 1)
            if key not in known:
                total = reaction + c_x[i] + c_x[i + 1] + c_south[bx] + c_north[bx] + c_below[bx] + c_above[bx]
                local = total + rob_y
                if i == 0:
                    local = local + p_x * inside[0]
                if i == cx - 1:
                    local = local + p_x * inside[1]
                inv = 1.0 / local
                west = zero if i == 0 else c_x[i] * inv
                east = zero if i == cx - 1 else c_x[i + 1] * inv
                known[key] = (
                    total, inv, west, east, loc_south[bx] * inv, loc_north[bx] * inv,
                    loc_below[bx] * inv, loc_above[bx] * inv,
                )
            return known[key]

        def set_planes(h):
            lo, hi = plane_terms(2 * h), plane_terms(2 * h + 1)
            diag_s[0, h] = lo[0]
            diag_s[1, h] = hi[0]
            for colour in range(2):
                low = even if colour == 0 else jnp.logical_not(even)
                coef[colour, 0, h] = jnp.where(low, lo[3], hi[2])
                coef[colour, 1, h] = jnp.where(low, lo[2], hi[3])
                for item in range(4):
                    coef[colour, 2 + item, h] = jnp.where(low, lo[4 + item], hi[4 + item])
                coef[colour, 6, h] = jnp.where(low, lo[1], hi[1])

        for h in range(1, half - 1):
            set_planes(h)
        pl.when(has[3])(row_south.wait_recv)
        pl.when(has[2])(row_north.wait_recv)
        if narrow > 2:
            pl.when(has[2] & has[3])(row_again.start)
        for side in (0, 1):
            @pl.when(has[side])
            def _(side=side):
                label_arrival(side).wait_recv()
        west_k = jnp.where(has[0], plane_of(kappa_rows(labels_in[0, blocks_x - 1])), kappa[0])
        east_k = jnp.where(has[1], plane_of(kappa_rows(labels_in[1, 0])), kappa[-1])
        c_x[0] = 0.5 * (west_k + kappa[0])
        c_x[cx] = 0.5 * (kappa[-1] + east_k)
        set_planes(0)
        set_planes(half - 1)
        if narrow > 2:
            pl.when(n + 2 < narrow)(row_again.wait_recv)
        pl.when(has[0])(column_west.start)
        pl.when(has[1])(column_east.start)
        loads[2].wait()

        def stacked(planes):
            return jnp.stack(planes, 0)

        def by_block(planes, parity):
            return stacked([planes[(2 * h + parity) // BLOCK] for h in range(half)])

        even3 = jnp.broadcast_to(even[None], (half, cy, nz))

        def packed(pair):
            return jnp.where(even3, pair[0], pair[1]), jnp.where(even3, pair[1], pair[0])

        def up(v):
            return jnp.concatenate([v[1:], v[:1]], 0)

        def down(v):
            return jnp.concatenate([v[-1:], v[:-1]], 0)

        def coupling(other, colour):
            if colour == 0:
                across = jnp.where(even3, down(other), up(other))
            else:
                across = jnp.where(even3, up(other), down(other))
            total = coef[colour, 0] * other + coef[colour, 1] * across
            total = total + coef[colour, 2] * pltpu.roll(other, 1, 1)
            total = total + coef[colour, 3] * pltpu.roll(other, cy - 1, 1)
            total = total + coef[colour, 4] * pltpu.roll(other, 1, 2)
            return total + coef[colour, 5] * pltpu.roll(other, nz - 1, 2)

        def relax(red, black, source):
            scaled = packed(source)
            scaled = (scaled[0] * coef[0, 6], scaled[1] * coef[1, 6])
            for sweep in range(SWEEPS):
                red = scaled[0] if black is None else scaled[0] + coupling(black, 0)
                black = scaled[1] + coupling(red, 1)
            return red, black

        right = tuple(stacked([rhs[2 * h + parity] for h in range(half)]) for parity in range(2))

        def misfit(u):
            result = []
            for parity in range(2):
                mine, other = u[parity], u[1 - parity]
                faces_w = stacked([zero if 2 * h + parity == 0 else c_x[2 * h + parity] for h in range(half)])
                faces_e = stacked(
                    [zero if 2 * h + parity == cx - 1 else c_x[2 * h + parity + 1] for h in range(half)]
                )
                west = down(other) if parity == 0 else other
                east = other if parity == 0 else up(other)
                total = right[parity] - diag_s[parity] * mine + faces_w * west + faces_e * east
                total = total + by_block(loc_south, parity) * pltpu.roll(mine, 1, 1)
                total = total + by_block(loc_north, parity) * pltpu.roll(mine, cy - 1, 1)
                total = total + by_block(loc_below, parity) * pltpu.roll(mine, 1, 2)
                total = total + by_block(loc_above, parity) * pltpu.roll(mine, nz - 1, 2)
                result.append(total)
            return result

        xi = [(i + 0.5) / cx for i in range(cx)]
        eta = (row_j.astype(f32) + 0.5) / cy
        eta_first, eta_last = 0.5 / cy, (cy - 0.5) / cy

        def weigh_x(pair):
            lows, highs = None, None
            for i in range(cx):
                plane = pair[i % 2][i // 2]
                low, high = (1.0 - xi[i]) * plane, xi[i] * plane
                lows = low if lows is None else lows + low
                highs = high if highs is None else highs + high
            return lows, highs

        win_row = lax.broadcasted_iota(jnp.int32, (16, count), 0)
        win_lane = lax.broadcasted_iota(jnp.int32, (16, count), 1)
        point_w = w + win_row // 4 - 1
        point_n = n + win_row % 4 - 1
        point_ok = (point_w >= 0) & (point_w < wide) & (point_n >= 0) & (point_n < narrow)
        point = jnp.where(point_ok, point_w * narrow + point_n, -1)
        at_point = point == win_lane
        slot_row = lax.broadcasted_iota(jnp.int32, (16, nz), 0)

        def edge_coef(planes, parity, row):
            return stacked([planes[(2 * h + parity) // BLOCK][row : row + 1] for h in range(half)])

        south_c = [edge_coef(c_south, parity, 0) * inside[2] for parity in range(2)]
        north_c = [edge_coef(c_north, parity, cy - 1) * inside[3] for parity in range(2)]
        west_c = c_x[0] * inside[0]
        east_c = c_x[cx] * inside[1]

        def restrict(u):
            low, high = weigh_x(misfit(u))
            out_w = west_c * u[0][0]
            out_e = east_c * u[1][half - 1]
            sums = {
                -1: (1.0 - xi[-1]) * out_w,
                0: low + xi[-1] * out_w,
                1: high + (1.0 - xi[0]) * out_e,
                2: xi[0] * out_e,
            }
            out_s = weigh_x([south_c[parity] * u[parity][:, 0:1] for parity in range(2)])
            out_n = weigh_x([north_c[parity] * u[parity][:, cy - 1 : cy] for parity in range(2)])
            table = jnp.zeros((16, nz), f32)
            for a in range(-1, 3):
                near = jnp.sum(sums[a] * (1.0 - eta), 0, keepdims=True)
                away = jnp.sum(sums[a] * eta, 0, keepdims=True)
                entries = {0: near, 1: away}
                if a in (0, 1):
                    entries[-1] = (1.0 - eta_last) * out_s[a]
                    entries[0] = near + eta_last * out_s[a]
                    entries[1] = away + (1.0 - eta_first) * out_n[a]
                    entries[2] = eta_first * out_n[a]
                for b, entry in entries.items():
                    table = jnp.where(slot_row == slot_at(a, b), jnp.broadcast_to(entry, (16, nz)), table)
            summed = jnp.sum(table, 1, keepdims=True)
            return jnp.sum(jnp.where(at_point, summed, 0.0), 0, keepdims=True)

        def face_copy(turn, side):
            dw, dn = SIDES[side]
            if side < 2:
                source, target = x_out.at[turn, side], x_in.at[turn, side ^ 1]
            else:
                source, target = y_out.at[turn, side - 2], y_in.at[turn, (side ^ 1) - 2]
            return pltpu.make_async_remote_copy(
                src_ref=source, dst_ref=target,
                send_sem=face_send.at[turn, side], recv_sem=face_recv.at[turn, side ^ 1],
                device_id=(w + dw, n + dn), device_id_type=MESH,
            )

        def face_arrival(turn, side):
            dw, dn = SIDES[side]
            if side < 2:
                source, target = x_out.at[turn, side], x_in.at[turn, side]
            else:
                source, target = y_out.at[turn, side - 2], y_in.at[turn, side - 2]
            return pltpu.make_async_remote_copy(
                src_ref=source, dst_ref=target,
                send_sem=face_send.at[turn, side], recv_sem=face_recv.at[turn, side],
                device_id=(w + dw, n + dn), device_id_type=MESH,
            )

        def spread_near(turn, dw, dn, rows):
            return pltpu.make_async_remote_copy(
                src_ref=near_sums.at[turn, rows], dst_ref=near_sums.at[turn, rows],
                send_sem=near_send.at[turn], recv_sem=near_recv.at[turn],
                device_id=near_peer(dw, dn), device_id_type=MESH,
            )

        def spread_far(turn, dw, rows):
            return pltpu.make_async_remote_copy(
                src_ref=far_sums.at[turn, rows], dst_ref=far_sums.at[turn, rows],
                send_sem=far_send.at[turn], recv_sem=far_recv.at[turn],
                device_id=far_peer(dw), device_id_type=MESH,
            )

        place = w_low * narrow + n
        all_near, all_far = pl.ds(0, group - 1), pl.ds(0, high - 1)

        red = black = None
        source = right
        for turn in range(ITERS):
            red, black = relax(red, black, source)
            u = [jnp.where(even3, red, black), jnp.where(even3, black, red)]
            x_out[turn, 0] = u[0][0]
            x_out[turn, 1] = u[1][half - 1]
            for parity in range(2):
                y_out[turn, 0, pl.ds(parity * half, half)] = u[parity][:, 0:1]
                y_out[turn, 1, pl.ds(parity * half, half)] = u[parity][:, cy - 1 : cy]
            for side in range(4):
                @pl.when(has[side])
                def _(turn=turn, side=side):
                    face_copy(turn, side).start()
            near_sums[turn, place] = restrict(u)
            for dw, dn in near:
                spread_near(turn, dw, dn, place).start()
            if turn == 0:
                pl.when(has[1])(column_west.wait_recv)
                pl.when(has[0])(column_east.wait_recv)
                pl.when(has[0] & has[1])(column_again.start)
            if near:
                spread_near(turn, 0, 1, all_near).wait_recv()
            far_sums[turn, w_high] = jnp.sum(near_sums[turn], 0)
            for dw in afar:
                spread_far(turn, dw, w_high).start()
            for side in range(4):
                @pl.when(has[side])
                def _(turn=turn, side=side):
                    face_arrival(turn, side).wait_recv()
            if turn == 0:
                pl.when(w + 2 < wide)(column_again.wait_recv)
            if afar:
                spread_far(turn, 1, all_far).wait_recv()
            load = jnp.sum(far_sums[turn], 0)
            value = {}
            for a, b in SLOTS:
                value[a, b] = jnp.sum(window[slot_at(a, b)] * load, 1, keepdims=True)

            along = {a: value[a, 0] * (1.0 - eta) + value[a, 1] * eta for a in range(-1, 3)}
            u = [
                u[parity]
                + stacked(
                    [
                        (1.0 - xi[2 * h + parity]) * along[0] + xi[2 * h + parity] * along[1]
                        for h in range(half)
                    ]
                )
                for parity in range(2)
            ]
            west_u = x_in[turn, 0] + (1.0 - xi[-1]) * along[-1] + xi[-1] * along[0]
            east_u = x_in[turn, 1] + (1.0 - xi[0]) * along[1] + xi[0] * along[2]
            under = [value[a, -1] * (1.0 - eta_last) + value[a, 0] * eta_last for a in (0, 1)]
            over = [value[a, 1] * (1.0 - eta_first) + value[a, 2] * eta_first for a in (0, 1)]

            def edge(base, ends, parity):
                return base + stacked(
                    [
                        jnp.broadcast_to(
                            (1.0 - xi[2 * h + parity]) * ends[0] + xi[2 * h + parity] * ends[1], (1, nz)
                        )
                        for h in range(half)
                    ]
                )

            south_u = [edge(y_in[turn, 0, pl.ds(parity * half, half)], under, parity) for parity in range(2)]
            north_u = [edge(y_in[turn, 1, pl.ds(parity * half, half)], over, parity) for parity in range(2)]
            out_x = [west_c * west_u, east_c * east_u]
            out_y = [[south_c[parity] * south_u[parity] for parity in range(2)],
                     [north_c[parity] * north_u[parity] for parity in range(2)]]
            last = turn + 1 == ITERS
            if not last:
                out_x[0] = out_x[0] + (inside[0] * p_x) * u[0][0]
                out_x[1] = out_x[1] + (inside[1] * p_x) * u[1][half - 1]
                for parity in range(2):
                    out_y[0][parity] = out_y[0][parity] + (inside[2] * p_y) * u[parity][:, 0:1]
                    out_y[1][parity] = out_y[1][parity] + (inside[3] * p_y) * u[parity][:, cy - 1 : cy]
            base = misfit(u) if last else right
            row3 = jnp.broadcast_to(row_j[None], (half, cy, nz))
            total = []
            for parity in range(2):
                ends = jnp.where(row3 == 0, jnp.broadcast_to(out_y[0][parity], row3.shape), 0.0)
                ends = jnp.where(row3 == cy - 1, jnp.broadcast_to(out_y[1][parity], row3.shape), ends)
                total.append(base[parity] + ends)
            total[0] = jnp.concatenate([total[0][:1] + out_x[0][None], total[0][1:]], 0)
            total[1] = jnp.concatenate([total[1][:-1], total[1][-1:] + out_x[1][None]], 0)
            if last:
                for i in range(cx):
                    sol_ref[i] = u[i % 2][i // 2].astype(jnp.bfloat16)
                    res_ref[i] = total[i % 2][i // 2].astype(jnp.bfloat16)
            else:
                source = total
                red, black = packed(u)

        for side in range(4):
            @pl.when(has[side])
            def _(side=side):
                label_copy(side).wait_send()
                for turn in range(ITERS):
                    face_copy(turn, side).wait_send()
        pl.when(has[2])(row_south.wait_send)
        pl.when(has[3])(row_north.wait_send)
        if narrow > 2:
            pl.when(has[2] & has[3])(row_again.wait_send)
        pl.when(has[0])(column_west.wait_send)
        pl.when(has[1])(column_east.wait_send)
        pl.when(has[0] & has[1])(column_again.wait_send)
        for turn in range(ITERS):
            if near:
                spread_near(turn, 0, 1, all_near).wait_send()
            if afar:
                spread_far(turn, 1, all_far).wait_send()

    scratch = [
        pltpu.VMEM(shape, f32),
        pltpu.VMEM(blocks, jnp.int32),
        pltpu.VMEM((4,) + blocks, jnp.int32),
        pltpu.VMEM((16, 1, count), f32),
        pltpu.VMEM((ITERS, group, 1, count), f32),
        pltpu.VMEM((ITERS, high, 1, count), f32),
        pltpu.VMEM((ITERS, 2, cy, nz), f32),
        pltpu.VMEM((ITERS, 2, cy, nz), f32),
        pltpu.VMEM((ITERS, 2, cx, 1, nz), f32),
        pltpu.VMEM((ITERS, 2, cx, 1, nz), f32),
        pltpu.VMEM((2, 7, half, cy, nz), f32),
        pltpu.VMEM((2, half, cy, nz), f32),
        pltpu.SemaphoreType.DMA((3,)),
        pltpu.SemaphoreType.DMA((4,)),
        pltpu.SemaphoreType.DMA((4,)),
        pltpu.SemaphoreType.DMA((4, 2)),
        pltpu.SemaphoreType.DMA((4, 2)),
        pltpu.SemaphoreType.DMA((ITERS, 4)),
        pltpu.SemaphoreType.DMA((ITERS, 4)),
        pltpu.SemaphoreType.DMA((ITERS,)),
        pltpu.SemaphoreType.DMA((ITERS,)),
        pltpu.SemaphoreType.DMA((ITERS,)),
        pltpu.SemaphoreType.DMA((ITERS,)),
    ]
    return kernel, scratch


def solution(mesh):
    wide, narrow = mesh.shape["wide"], mesh.shape["narrow"]

    def body(right_side, labels, material_table, robin_table, robin_index, coarse_rows):
        shape = right_side.shape
        kernel, scratch = make_kernel(wide, narrow, shape, labels.shape)
        anywhere = pl.BlockSpec(memory_space=pl.ANY)
        scalars = pl.BlockSpec(memory_space=pltpu.SMEM)
        vectors = pl.BlockSpec(memory_space=pltpu.VMEM)
        return pl.pallas_call(
            kernel,
            out_shape=(jax.ShapeDtypeStruct(shape, jnp.bfloat16),) * 2,
            in_specs=[anywhere, anywhere, scalars, scalars, scalars, anywhere],
            out_specs=(vectors, vectors),
            scratch_shapes=scratch,
            compiler_params=pltpu.CompilerParams(collective_id=0, has_side_effects=True),
        )(right_side, labels, material_table, robin_table, robin_index, coarse_rows)

    cells = P("wide", "narrow", None)
    return jax.shard_map(
        body,
        mesh=mesh,
        in_specs=(cells, cells, P(), P(), cells, P(("wide", "narrow"), None)),
        out_specs=(cells, cells),
        check_vma=False,
    )
```

```python
import jax
import jax.numpy as jnp
from jax import lax
from jax.experimental import pallas as pl
from jax.experimental.pallas import tpu as pltpu
from jax.sharding import PartitionSpec as P

BLOCK = 8
SWEEPS = 4
ITERS = 2
reaction = 1.0
MESH = pl.DeviceIdType.MESH
SIDES = ((-1, 0), (1, 0), (0, -1), (0, 1))
SLOTS = [(a, b) for a in range(-1, 3) for b in range(-1, 3) if a in (0, 1) or b in (0, 1)]


def slot_at(a, b):
    return 4 * (a + 1) + (b + 1)


def make_kernel(wide, narrow, shape, blocks, tables):
    cx, cy, nz = shape
    half = cx // 2
    count = wide * narrow
    paired = wide & (wide - 1) == 0 and narrow & (narrow - 1) == 0
    bits = [(1 << k, 0) for k in reversed(range(wide.bit_length() - 1))]
    bits += [(0, 1 << k) for k in range(narrow.bit_length() - 1)]
    others = [(dw, dn) for dw in range(wide) for dn in range(narrow) if dw or dn]
    others.sort(key=lambda by: (abs(by[0] - wide // 2), -by[1]))
    blocks_x, blocks_y, blocks_z = blocks
    f32 = jnp.float32

    def kernel(
        rhs_hbm, labels_hbm, material_hbm, robin_hbm, index_hbm, rows_hbm,
        sol_ref, res_ref,
        material, robin_table, robin_index, rhs, labels, labels_in, window, sums, x_out, x_in, y_out, y_in, coef, diag_s,
        local_sem, label_send, label_recv, row_send, row_recv,
        face_send, face_recv, sum_send, sum_recv, known_sem,
    ):
        w = lax.axis_index("wide")
        n = lax.axis_index("narrow")
        loads = [
            pltpu.make_async_copy(labels_hbm, labels, local_sem.at[0]),
            pltpu.make_async_copy(rows_hbm, window.at[slot_at(0, 0)], local_sem.at[1]),
            pltpu.make_async_copy(rhs_hbm, rhs, local_sem.at[2]),
            pltpu.make_async_copy(material_hbm, material, local_sem.at[3]),
            pltpu.make_async_copy(robin_hbm, robin_table, local_sem.at[4]),
            pltpu.make_async_copy(index_hbm, robin_index, local_sem.at[5]),
        ]
        labels_in[...] = jnp.zeros_like(labels_in)
        x_in[...] = jnp.zeros_like(x_in)
        y_in[...] = jnp.zeros_like(y_in)
        for slot in range(16):
            if slot != slot_at(0, 0):
                window[slot] = jnp.zeros_like(window[slot])
        for load in loads:
            load.start()
        barrier = pltpu.get_barrier_semaphore()

        has = [w > 0, w < wide - 1, n > 0, n < narrow - 1]
        me = w * narrow + n

        def flipped(at, bit):
            return at + bit - 2 * bit * (at // bit % 2) if bit else at

        def partner(stage):
            return (flipped(w, bits[stage][0]), flipped(n, bits[stage][1]))

        def signal(sem, target):
            pl.semaphore_signal(sem, inc=1, device_id=target, device_id_type=MESH)

        if paired:
            for side in range(4):
                @pl.when(has[side])
                def _(side=side):
                    signal(barrier, (w + SIDES[side][0], n + SIDES[side][1]))
            greeted = sum(jnp.where(flag, 1, 0) for flag in has) + len(bits)
            for stage in range(len(bits)):
                signal(barrier, partner(stage))
        else:
            for dw, dn in others:
                signal(barrier, ((w + dw) % wide, (n + dn) % narrow))
            greeted = len(others)
        stages = iter(range(len(bits)))

        def begin_stage():
            signal(known_sem.at[0], partner(0))

        def next_stage():
            stage = next(stages, None)
            if paired and stage is not None:
                pl.semaphore_wait(known_sem.at[stage], 1)
                if stage + 1 < len(bits):
                    signal(known_sem.at[stage + 1], partner(stage + 1))
            return stage is not None

        inside = [jnp.where(flag, 1.0, 0.0).astype(f32) for flag in has]
        spread = (
            lax.broadcasted_iota(jnp.int32, (blocks_z, nz), 1) // BLOCK
            == lax.broadcasted_iota(jnp.int32, (blocks_z, nz), 0)
        ).astype(f32)
        row_j = lax.broadcasted_iota(jnp.int32, (cy, nz), 0)
        lane_k = lax.broadcasted_iota(jnp.int32, (cy, nz), 1)
        even = (row_j + lane_k) % 2 == 0

        def kappa_rows(label_rows):
            wide_rows = jnp.dot(label_rows.astype(f32), spread, preferred_element_type=f32)
            found = jnp.zeros_like(wide_rows)
            for entry in range(material.shape[0]):
                found = jnp.where(wide_rows == float(entry), material[entry], found)
            return found

        def plane_of(rows):
            plane = jnp.broadcast_to(rows[blocks_y - 1 : blocks_y], (cy, nz))
            for at in range(blocks_y - 2, -1, -1):
                plane = jnp.where(row_j < (at + 1) * BLOCK, jnp.broadcast_to(rows[at : at + 1], (cy, nz)), plane)
            return plane

        for at in (0, 1, 3, 4, 5):
            loads[at].wait()
        p_x = robin_table[robin_index[0, 0, 0]]
        p_y = robin_table[robin_index[0, 0, 1]]

        kappa = [plane_of(kappa_rows(labels[bx])) for bx in range(blocks_x)]
        c_below, c_above = [], []
        for plane in kappa:
            c_below.append(0.5 * (plane + jnp.where(lane_k == 0, plane, pltpu.roll(plane, 1, 1))))
            c_above.append(0.5 * (plane + jnp.where(lane_k == nz - 1, plane, pltpu.roll(plane, nz - 1, 1))))

        pl.semaphore_wait(barrier, greeted)

        def label_copy(side):
            dw, dn = SIDES[side]
            return pltpu.make_async_remote_copy(
                src_ref=labels, dst_ref=labels_in.at[side ^ 1],
                send_sem=label_send.at[side], recv_sem=label_recv.at[side ^ 1],
                device_id=(w + dw, n + dn), device_id_type=MESH,
            )

        def label_arrival(side):
            dw, dn = SIDES[side]
            return pltpu.make_async_remote_copy(
                src_ref=labels, dst_ref=labels_in.at[side],
                send_sem=label_send.at[side], recv_sem=label_recv.at[side],
                device_id=(w + dw, n + dn), device_id_type=MESH,
            )

        for side in range(4):
            @pl.when(has[side])
            def _(side=side):
                label_copy(side).start()

        def row_step(kind, at, source, target, dw, dn):
            return pltpu.make_async_remote_copy(
                src_ref=source, dst_ref=target, send_sem=row_send.at[kind, at], recv_sem=row_recv.at[kind, at],
                device_id=(w + dw, n + dn), device_id_type=MESH,
            )

        def column(a):
            return window.at[pl.ds(4 * (a + 1), 4)]

        own_row = window.at[slot_at(0, 0)]
        row_south = row_step(0, 0, own_row, window.at[slot_at(0, 1)], 0, -1)
        row_north = row_step(0, 1, own_row, window.at[slot_at(0, -1)], 0, 1)
        row_again = row_step(1, 0, window.at[slot_at(0, 1)], window.at[slot_at(0, 2)], 0, -1)
        column_west = row_step(2, 0, column(0), column(1), -1, 0)
        column_east = row_step(2, 1, column(0), column(-1), 1, 0)
        column_again = row_step(3, 0, column(1), column(2), -1, 0)
        pl.when(has[2])(row_south.start)
        pl.when(has[3])(row_north.start)

        if paired and bits:
            begin_stage()
        for side in (2, 3):
            @pl.when(has[side])
            def _(side=side):
                label_arrival(side).wait_recv()
        next_stage()

        c_south, c_north = [], []
        for bx in range(blocks_x):
            plane = kappa[bx]
            south_row = jnp.broadcast_to(kappa_rows(labels_in[2, bx])[blocks_y - 1 : blocks_y], (cy, nz))
            north_row = jnp.broadcast_to(kappa_rows(labels_in[3, bx])[0:1], (cy, nz))
            below = jnp.where(has[2], south_row, plane)
            above = jnp.where(has[3], north_row, plane)
            c_south.append(0.5 * (plane + jnp.where(row_j == 0, below, pltpu.roll(plane, 1, 0))))
            c_north.append(0.5 * (plane + jnp.where(row_j == cy - 1, above, pltpu.roll(plane, cy - 1, 0))))

        between = [0.5 * (kappa[bx] + kappa[bx + 1]) for bx in range(blocks_x - 1)]
        c_x = [
            kappa[i // BLOCK] if i % BLOCK else between[i // BLOCK - 1] if 0 < i < cx else None
            for i in range(cx + 1)
        ]

        zero = jnp.zeros((cy, nz), f32)
        loc_south = [jnp.where(row_j == 0, 0.0, c) for c in c_south]
        loc_north = [jnp.where(row_j == cy - 1, 0.0, c) for c in c_north]
        loc_below = [jnp.where(lane_k == 0, 0.0, c) for c in c_below]
        loc_above = [jnp.where(lane_k == nz - 1, 0.0, c) for c in c_above]
        rob_y = p_y * (inside[2] * (row_j == 0).astype(f32) + inside[3] * (row_j == cy - 1).astype(f32))
        known = {}

        def plane_terms(i):
            bx = i // BLOCK
            key = (bx, i % BLOCK == 0, i % BLOCK == BLOCK - 1)
            if key not in known:
                total = reaction + c_x[i] + c_x[i + 1] + c_south[bx] + c_north[bx] + c_below[bx] + c_above[bx]
                local = total + rob_y
                if i == 0:
                    local = local + p_x * inside[0]
                if i == cx - 1:
                    local = local + p_x * inside[1]
                inv = 1.0 / local
                west = zero if i == 0 else c_x[i] * inv
                east = zero if i == cx - 1 else c_x[i + 1] * inv
                known[key] = (
                    total, inv, west, east, loc_south[bx] * inv, loc_north[bx] * inv,
                    loc_below[bx] * inv, loc_above[bx] * inv,
                )
            return known[key]

        def set_planes(h):
            lo, hi = plane_terms(2 * h), plane_terms(2 * h + 1)
            diag_s[0, h] = lo[0]
            diag_s[1, h] = hi[0]
            for colour in range(2):
                low = even if colour == 0 else jnp.logical_not(even)
                coef[colour, 0, h] = jnp.where(low, lo[3], hi[2])
                coef[colour, 1, h] = jnp.where(low, lo[2], hi[3])
                for item in range(4):
                    coef[colour, 2 + item, h] = jnp.where(low, lo[4 + item], hi[4 + item])
                coef[colour, 6, h] = jnp.where(low, lo[1], hi[1])

        for h in range(1, half - 1):
            set_planes(h)
        next_stage()
        pl.when(has[3])(row_south.wait_recv)
        pl.when(has[2])(row_north.wait_recv)
        if narrow > 2:
            pl.when(has[2] & has[3])(row_again.start)
        for side in (0, 1):
            @pl.when(has[side])
            def _(side=side):
                label_arrival(side).wait_recv()
        next_stage()
        west_k = jnp.where(has[0], plane_of(kappa_rows(labels_in[0, blocks_x - 1])), kappa[0])
        east_k = jnp.where(has[1], plane_of(kappa_rows(labels_in[1, 0])), kappa[-1])
        c_x[0] = 0.5 * (west_k + kappa[0])
        c_x[cx] = 0.5 * (kappa[-1] + east_k)
        set_planes(0)
        set_planes(half - 1)
        if narrow > 2:
            pl.when(n + 2 < narrow)(row_again.wait_recv)
        pl.when(has[0])(column_west.start)
        pl.when(has[1])(column_east.start)
        next_stage()
        loads[2].wait()

        def stacked(planes):
            return jnp.stack(planes, 0)

        def by_block(planes, parity):
            return stacked([planes[(2 * h + parity) // BLOCK] for h in range(half)])

        even3 = jnp.broadcast_to(even[None], (half, cy, nz))

        def packed(pair):
            return jnp.where(even3, pair[0], pair[1]), jnp.where(even3, pair[1], pair[0])

        def up(v):
            return jnp.concatenate([v[1:], v[:1]], 0)

        def down(v):
            return jnp.concatenate([v[-1:], v[:-1]], 0)

        def coupling(other, colour):
            if colour == 0:
                across = jnp.where(even3, down(other), up(other))
            else:
                across = jnp.where(even3, up(other), down(other))
            total = coef[colour, 0] * other + coef[colour, 1] * across
            total = total + coef[colour, 2] * pltpu.roll(other, 1, 1)
            total = total + coef[colour, 3] * pltpu.roll(other, cy - 1, 1)
            total = total + coef[colour, 4] * pltpu.roll(other, 1, 2)
            return total + coef[colour, 5] * pltpu.roll(other, nz - 1, 2)

        def relax(red, black, source):
            scaled = packed(source)
            scaled = (scaled[0] * coef[0, 6], scaled[1] * coef[1, 6])
            for sweep in range(SWEEPS):
                red = scaled[0] if black is None else scaled[0] + coupling(black, 0)
                black = scaled[1] + coupling(red, 1)
            return red, black

        right = tuple(stacked([rhs[2 * h + parity] for h in range(half)]) for parity in range(2))

        def misfit(u):
            result = []
            for parity in range(2):
                mine, other = u[parity], u[1 - parity]
                faces_w = stacked([zero if 2 * h + parity == 0 else c_x[2 * h + parity] for h in range(half)])
                faces_e = stacked(
                    [zero if 2 * h + parity == cx - 1 else c_x[2 * h + parity + 1] for h in range(half)]
                )
                west = down(other) if parity == 0 else other
                east = other if parity == 0 else up(other)
                total = right[parity] - diag_s[parity] * mine + faces_w * west + faces_e * east
                total = total + by_block(loc_south, parity) * pltpu.roll(mine, 1, 1)
                total = total + by_block(loc_north, parity) * pltpu.roll(mine, cy - 1, 1)
                total = total + by_block(loc_below, parity) * pltpu.roll(mine, 1, 2)
                total = total + by_block(loc_above, parity) * pltpu.roll(mine, nz - 1, 2)
                result.append(total)
            return result

        xi = [(i + 0.5) / cx for i in range(cx)]
        eta = (row_j.astype(f32) + 0.5) / cy
        eta_first, eta_last = 0.5 / cy, (cy - 0.5) / cy

        def weigh_x(pair):
            lows, highs = None, None
            for i in range(cx):
                plane = pair[i % 2][i // 2]
                low, high = (1.0 - xi[i]) * plane, xi[i] * plane
                lows = low if lows is None else lows + low
                highs = high if highs is None else highs + high
            return lows, highs

        win_row = lax.broadcasted_iota(jnp.int32, (16, count), 0)
        win_lane = lax.broadcasted_iota(jnp.int32, (16, count), 1)
        point_w = w + win_row // 4 - 1
        point_n = n + win_row % 4 - 1
        point_ok = (point_w >= 0) & (point_w < wide) & (point_n >= 0) & (point_n < narrow)
        point = jnp.where(point_ok, point_w * narrow + point_n, -1)
        at_point = point == win_lane
        slot_row = lax.broadcasted_iota(jnp.int32, (16, nz), 0)

        def edge_coef(planes, parity, row):
            return stacked([planes[(2 * h + parity) // BLOCK][row : row + 1] for h in range(half)])

        south_c = [edge_coef(c_south, parity, 0) * inside[2] for parity in range(2)]
        north_c = [edge_coef(c_north, parity, cy - 1) * inside[3] for parity in range(2)]
        west_c = c_x[0] * inside[0]
        east_c = c_x[cx] * inside[1]

        def restrict(u):
            low, high = weigh_x(misfit(u))
            out_w = west_c * u[0][0]
            out_e = east_c * u[1][half - 1]
            sums = {
                -1: (1.0 - xi[-1]) * out_w,
                0: low + xi[-1] * out_w,
                1: high + (1.0 - xi[0]) * out_e,
                2: xi[0] * out_e,
            }
            out_s = weigh_x([south_c[parity] * u[parity][:, 0:1] for parity in range(2)])
            out_n = weigh_x([north_c[parity] * u[parity][:, cy - 1 : cy] for parity in range(2)])
            table = jnp.zeros((16, nz), f32)
            for a in range(-1, 3):
                near = jnp.sum(sums[a] * (1.0 - eta), 0, keepdims=True)
                away = jnp.sum(sums[a] * eta, 0, keepdims=True)
                entries = {0: near, 1: away}
                if a in (0, 1):
                    entries[-1] = (1.0 - eta_last) * out_s[a]
                    entries[0] = near + eta_last * out_s[a]
                    entries[1] = away + (1.0 - eta_first) * out_n[a]
                    entries[2] = eta_first * out_n[a]
                for b, entry in entries.items():
                    table = jnp.where(slot_row == slot_at(a, b), jnp.broadcast_to(entry, (16, nz)), table)
            summed = jnp.sum(table, 1, keepdims=True)
            return jnp.sum(jnp.where(at_point, summed, 0.0), 0, keepdims=True)

        def face_copy(turn, side):
            dw, dn = SIDES[side]
            if side < 2:
                source, target = x_out.at[turn, side], x_in.at[turn, side ^ 1]
            else:
                source, target = y_out.at[turn, side - 2], y_in.at[turn, (side ^ 1) - 2]
            return pltpu.make_async_remote_copy(
                src_ref=source, dst_ref=target,
                send_sem=face_send.at[turn, side], recv_sem=face_recv.at[turn, side ^ 1],
                device_id=(w + dw, n + dn), device_id_type=MESH,
            )

        def face_arrival(turn, side):
            dw, dn = SIDES[side]
            if side < 2:
                source, target = x_out.at[turn, side], x_in.at[turn, side]
            else:
                source, target = y_out.at[turn, side - 2], y_in.at[turn, side - 2]
            return pltpu.make_async_remote_copy(
                src_ref=source, dst_ref=target,
                send_sem=face_send.at[turn, side], recv_sem=face_recv.at[turn, side],
                device_id=(w + dw, n + dn), device_id_type=MESH,
            )

        def spread_sum(turn, dw, dn, rows):
            return pltpu.make_async_remote_copy(
                src_ref=sums.at[turn, rows], dst_ref=sums.at[turn, rows],
                send_sem=sum_send.at[turn], recv_sem=sum_recv.at[turn],
                device_id=((w + dw) % wide, (n + dn) % narrow), device_id_type=MESH,
            )

        received = pl.ds(0, count - 1)

        red = black = None
        source = right
        for turn in range(ITERS):
            red, black = relax(red, black, source)
            u = [jnp.where(even3, red, black), jnp.where(even3, black, red)]
            x_out[turn, 0] = u[0][0]
            x_out[turn, 1] = u[1][half - 1]
            for parity in range(2):
                y_out[turn, 0, pl.ds(parity * half, half)] = u[parity][:, 0:1]
                y_out[turn, 1, pl.ds(parity * half, half)] = u[parity][:, cy - 1 : cy]
            for side in range(4):
                @pl.when(has[side])
                def _(turn=turn, side=side):
                    face_copy(turn, side).start()
            sums[turn, me] = restrict(u)
            while next_stage():
                pass
            if count <= 64:
                for dw, dn in others:
                    spread_sum(turn, dw, dn, me).start()
            else:
                def scatter(step, carry, turn=turn):
                    flat = (me + step) % count
                    spread_sum(turn, flat // narrow + wide - w, flat % narrow + narrow - n, me).start()
                    return carry

                lax.fori_loop(1, count, scatter, 0)
            if turn == 0:
                pl.when(has[1])(column_west.wait_recv)
                pl.when(has[0])(column_east.wait_recv)
                pl.when(has[0] & has[1])(column_again.start)
            for side in range(4):
                @pl.when(has[side])
                def _(turn=turn, side=side):
                    face_arrival(turn, side).wait_recv()
            if turn == 0:
                pl.when(w + 2 < wide)(column_again.wait_recv)
            if others:
                spread_sum(turn, *others[0], received).wait_recv()
            load = jnp.sum(sums[turn], 0)
            value = {}
            for a, b in SLOTS:
                value[a, b] = jnp.sum(window[slot_at(a, b)] * load, 1, keepdims=True)

            along = {a: value[a, 0] * (1.0 - eta) + value[a, 1] * eta for a in range(-1, 3)}
            u = [
                u[parity]
                + stacked(
                    [
                        (1.0 - xi[2 * h + parity]) * along[0] + xi[2 * h + parity] * along[1]
                        for h in range(half)
                    ]
                )
                for parity in range(2)
            ]
            west_u = x_in[turn, 0] + (1.0 - xi[-1]) * along[-1] + xi[-1] * along[0]
            east_u = x_in[turn, 1] + (1.0 - xi[0]) * along[1] + xi[0] * along[2]
            under = [value[a, -1] * (1.0 - eta_last) + value[a, 0] * eta_last for a in (0, 1)]
            over = [value[a, 1] * (1.0 - eta_first) + value[a, 2] * eta_first for a in (0, 1)]

            def edge(base, ends, parity):
                return base + stacked(
                    [
                        jnp.broadcast_to(
                            (1.0 - xi[2 * h + parity]) * ends[0] + xi[2 * h + parity] * ends[1], (1, nz)
                        )
                        for h in range(half)
                    ]
                )

            south_u = [edge(y_in[turn, 0, pl.ds(parity * half, half)], under, parity) for parity in range(2)]
            north_u = [edge(y_in[turn, 1, pl.ds(parity * half, half)], over, parity) for parity in range(2)]
            out_x = [west_c * west_u, east_c * east_u]
            out_y = [[south_c[parity] * south_u[parity] for parity in range(2)],
                     [north_c[parity] * north_u[parity] for parity in range(2)]]
            last = turn + 1 == ITERS
            if not last:
                out_x[0] = out_x[0] + (inside[0] * p_x) * u[0][0]
                out_x[1] = out_x[1] + (inside[1] * p_x) * u[1][half - 1]
                for parity in range(2):
                    out_y[0][parity] = out_y[0][parity] + (inside[2] * p_y) * u[parity][:, 0:1]
                    out_y[1][parity] = out_y[1][parity] + (inside[3] * p_y) * u[parity][:, cy - 1 : cy]
            base = misfit(u) if last else right
            row3 = jnp.broadcast_to(row_j[None], (half, cy, nz))
            total = []
            for parity in range(2):
                ends = jnp.where(row3 == 0, jnp.broadcast_to(out_y[0][parity], row3.shape), 0.0)
                ends = jnp.where(row3 == cy - 1, jnp.broadcast_to(out_y[1][parity], row3.shape), ends)
                total.append(base[parity] + ends)
            total[0] = jnp.concatenate([total[0][:1] + out_x[0][None], total[0][1:]], 0)
            total[1] = jnp.concatenate([total[1][:-1], total[1][-1:] + out_x[1][None]], 0)
            if last:
                for i in range(cx):
                    sol_ref[i] = u[i % 2][i // 2].astype(jnp.bfloat16)
                    res_ref[i] = total[i % 2][i // 2].astype(jnp.bfloat16)
            else:
                source = total
                red, black = packed(u)

        for side in range(4):
            @pl.when(has[side])
            def _(side=side):
                label_copy(side).wait_send()
                for turn in range(ITERS):
                    face_copy(turn, side).wait_send()
        pl.when(has[2])(row_south.wait_send)
        pl.when(has[3])(row_north.wait_send)
        if narrow > 2:
            pl.when(has[2] & has[3])(row_again.wait_send)
        pl.when(has[0])(column_west.wait_send)
        pl.when(has[1])(column_east.wait_send)
        pl.when(has[0] & has[1])(column_again.wait_send)
        for turn in range(ITERS):
            if others:
                spread_sum(turn, *others[0], received).wait_send()

    scratch = [
        pltpu.SMEM(tables[0], f32),
        pltpu.SMEM(tables[1], f32),
        pltpu.SMEM(tables[2], jnp.int32),
        pltpu.VMEM(shape, f32),
        pltpu.VMEM(blocks, jnp.int32),
        pltpu.VMEM((4,) + blocks, jnp.int32),
        pltpu.VMEM((16, 1, count), f32),
        pltpu.VMEM((ITERS, count, 1, count), f32),
        pltpu.VMEM((ITERS, 2, cy, nz), f32),
        pltpu.VMEM((ITERS, 2, cy, nz), f32),
        pltpu.VMEM((ITERS, 2, cx, 1, nz), f32),
        pltpu.VMEM((ITERS, 2, cx, 1, nz), f32),
        pltpu.VMEM((2, 7, half, cy, nz), f32),
        pltpu.VMEM((2, half, cy, nz), f32),
        pltpu.SemaphoreType.DMA((6,)),
        pltpu.SemaphoreType.DMA((4,)),
        pltpu.SemaphoreType.DMA((4,)),
        pltpu.SemaphoreType.DMA((4, 2)),
        pltpu.SemaphoreType.DMA((4, 2)),
        pltpu.SemaphoreType.DMA((ITERS, 4)),
        pltpu.SemaphoreType.DMA((ITERS, 4)),
        pltpu.SemaphoreType.DMA((ITERS,)),
        pltpu.SemaphoreType.DMA((ITERS,)),
        pltpu.SemaphoreType.REGULAR((max(1, len(bits)),)),
    ]
    return kernel, scratch


def solution(mesh):
    wide, narrow = mesh.shape["wide"], mesh.shape["narrow"]

    def body(right_side, labels, material_table, robin_table, robin_index, coarse_rows):
        shape = right_side.shape
        kernel, scratch = make_kernel(
            wide, narrow, shape, labels.shape, (material_table.shape, robin_table.shape, robin_index.shape)
        )
        anywhere = pl.BlockSpec(memory_space=pl.ANY)
        vectors = pl.BlockSpec(memory_space=pltpu.VMEM)
        return pl.pallas_call(
            kernel,
            out_shape=(pltpu.VMEM(shape, jnp.bfloat16),) * 2,
            in_specs=[anywhere] * 6,
            out_specs=(vectors, vectors),
            scratch_shapes=scratch,
            compiler_params=pltpu.CompilerParams(collective_id=0, has_side_effects=True),
        )(right_side, labels, material_table, robin_table, robin_index, coarse_rows)

    cells = P("wide", "narrow", None)
    return jax.shard_map(
        body,
        mesh=mesh,
        in_specs=(cells, cells, P(), P(), cells, P(("wide", "narrow"), None)),
        out_specs=(cells, cells),
        check_vma=False,
    )
```

```python
import jax
import jax.numpy as jnp
from jax import lax
from jax.experimental import pallas as pl
from jax.experimental.pallas import tpu as pltpu
from jax.sharding import PartitionSpec as P

BLOCK = 8
SWEEPS = 4
ITERS = 2
reaction = 1.0
MESH = pl.DeviceIdType.MESH
SIDES = ((-1, 0), (1, 0), (0, -1), (0, 1))
SLOTS = [(a, b) for a in range(-1, 3) for b in range(-1, 3) if a in (0, 1) or b in (0, 1)]


def slot_at(a, b):
    return 4 * (a + 1) + (b + 1)


def make_kernel(wide, narrow, shape, blocks, tables):
    cx, cy, nz = shape
    half = cx // 2
    count = wide * narrow
    paired = wide & (wide - 1) == 0 and narrow & (narrow - 1) == 0
    bits = [(1 << k, 0) for k in reversed(range(wide.bit_length() - 1))]
    bits += [(0, 1 << k) for k in range(narrow.bit_length() - 1)]
    others = [(dw, dn) for dw in range(wide) for dn in range(narrow) if dw or dn]
    others.sort(key=lambda by: (abs(by[0] - wide // 2), -by[1]))
    blocks_x, blocks_y, blocks_z = blocks
    f32 = jnp.float32

    def kernel(
        rhs_hbm, labels_hbm, material_hbm, robin_hbm, index_hbm, rows_hbm,
        sol_ref, res_ref,
        material, robin_table, robin_index, rhs, labels, labels_in, window, gathered, x_out, x_in, y_out, y_in, coef, diag_s,
        local_sem, label_send, label_recv, row_send, row_recv,
        face_send, face_recv, gather_send, gather_recv, known_sem,
    ):
        w = lax.axis_index("wide")
        n = lax.axis_index("narrow")
        me = w * narrow + n
        loads = [
            pltpu.make_async_copy(labels_hbm, labels, local_sem.at[0]),
            pltpu.make_async_copy(rows_hbm, window.at[slot_at(0, 0)], local_sem.at[1]),
            pltpu.make_async_copy(rhs_hbm, rhs, local_sem.at[2]),
            pltpu.make_async_copy(material_hbm, material, local_sem.at[3]),
            pltpu.make_async_copy(robin_hbm, robin_table, local_sem.at[4]),
            pltpu.make_async_copy(index_hbm, robin_index, local_sem.at[5]),
        ]
        labels_in[...] = jnp.zeros_like(labels_in)
        x_in[...] = jnp.zeros_like(x_in)
        y_in[...] = jnp.zeros_like(y_in)
        for a, b in SLOTS:
            if (a, b) != (0, 0):
                window[slot_at(a, b)] = jnp.zeros_like(window[slot_at(a, b)])
        for load in loads:
            load.start()
        barrier = pltpu.get_barrier_semaphore()

        def peer(step):
            flat = me + step
            flat = jnp.where(flat >= count, flat - count, flat)
            return (flat // narrow, flat % narrow)

        has = [w > 0, w < wide - 1, n > 0, n < narrow - 1]

        def flipped(at, bit):
            return at + bit - 2 * bit * (at // bit % 2) if bit else at

        def partner(stage):
            return (flipped(w, bits[stage][0]), flipped(n, bits[stage][1]))

        def signal(sem, target):
            pl.semaphore_signal(sem, inc=1, device_id=target, device_id_type=MESH)

        if paired:
            for side in range(4):
                @pl.when(has[side])
                def _(side=side):
                    signal(barrier, (w + SIDES[side][0], n + SIDES[side][1]))
            greeted = sum(jnp.where(flag, 1, 0) for flag in has) + len(bits)
            for stage in range(len(bits)):
                signal(barrier, partner(stage))
        else:
            for dw, dn in others:
                signal(barrier, ((w + dw) % wide, (n + dn) % narrow))
            greeted = len(others)
        stages = iter(range(len(bits)))

        def begin_stage():
            signal(known_sem.at[0], partner(0))

        def next_stage():
            stage = next(stages, None)
            if paired and stage is not None:
                pl.semaphore_wait(known_sem.at[stage], 1)
                if stage + 1 < len(bits):
                    signal(known_sem.at[stage + 1], partner(stage + 1))
            return stage is not None

        inside = [jnp.where(flag, 1.0, 0.0).astype(f32) for flag in has]
        spread = (
            lax.broadcasted_iota(jnp.int32, (blocks_z, nz), 1) // BLOCK
            == lax.broadcasted_iota(jnp.int32, (blocks_z, nz), 0)
        ).astype(f32)
        row_j = lax.broadcasted_iota(jnp.int32, (cy, nz), 0)
        lane_k = lax.broadcasted_iota(jnp.int32, (cy, nz), 1)
        even = (row_j + lane_k) % 2 == 0

        def kappa_rows(label_rows):
            wide_rows = jnp.dot(label_rows.astype(f32), spread, preferred_element_type=f32)
            found = jnp.zeros_like(wide_rows)
            for entry in range(material.shape[0]):
                found = jnp.where(wide_rows == float(entry), material[entry], found)
            return found

        def plane_of(rows):
            plane = jnp.broadcast_to(rows[blocks_y - 1 : blocks_y], (cy, nz))
            for at in range(blocks_y - 2, -1, -1):
                plane = jnp.where(row_j < (at + 1) * BLOCK, jnp.broadcast_to(rows[at : at + 1], (cy, nz)), plane)
            return plane

        for at in (0, 1, 3, 4, 5):
            loads[at].wait()
        p_x = robin_table[robin_index[0, 0, 0]]
        p_y = robin_table[robin_index[0, 0, 1]]

        kappa = [plane_of(kappa_rows(labels[bx])) for bx in range(blocks_x)]
        c_below, c_above = [], []
        for plane in kappa:
            c_below.append(0.5 * (plane + jnp.where(lane_k == 0, plane, pltpu.roll(plane, 1, 1))))
            c_above.append(0.5 * (plane + jnp.where(lane_k == nz - 1, plane, pltpu.roll(plane, nz - 1, 1))))

        pl.semaphore_wait(barrier, greeted)

        def label_copy(side):
            dw, dn = SIDES[side]
            return pltpu.make_async_remote_copy(
                src_ref=labels, dst_ref=labels_in.at[side ^ 1],
                send_sem=label_send.at[side], recv_sem=label_recv.at[side ^ 1],
                device_id=(w + dw, n + dn), device_id_type=MESH,
            )

        def label_arrival(side):
            dw, dn = SIDES[side]
            return pltpu.make_async_remote_copy(
                src_ref=labels, dst_ref=labels_in.at[side],
                send_sem=label_send.at[side], recv_sem=label_recv.at[side],
                device_id=(w + dw, n + dn), device_id_type=MESH,
            )

        for side in range(4):
            @pl.when(has[side])
            def _(side=side):
                label_copy(side).start()

        def on_grid(a, b):
            return (w + a >= 0) & (w + a < wide) & (n + b >= 0) & (n + b < narrow)

        def row_copy(a, b):
            slot = slot_at(a, b)
            return pltpu.make_async_remote_copy(
                src_ref=window.at[slot_at(0, 0)], dst_ref=window.at[slot],
                send_sem=row_send.at[slot], recv_sem=row_recv.at[slot],
                device_id=(w - a, n - b), device_id_type=MESH,
            )

        far = [(a, b) for a, b in SLOTS if (a, b) != (0, 0) and abs(a) < wide and abs(b) < narrow]
        if paired and bits:
            begin_stage()
            next_stage()
            next_stage()
        loads[2].wait()
        for side in range(4):
            @pl.when(has[side])
            def _(side=side):
                label_arrival(side).wait_recv()

        next_stage()
        west_k = jnp.where(has[0], plane_of(kappa_rows(labels_in[0, blocks_x - 1])), kappa[0])
        east_k = jnp.where(has[1], plane_of(kappa_rows(labels_in[1, 0])), kappa[-1])
        c_south, c_north = [], []
        for bx in range(blocks_x):
            plane = kappa[bx]
            south_row = jnp.broadcast_to(kappa_rows(labels_in[2, bx])[blocks_y - 1 : blocks_y], (cy, nz))
            north_row = jnp.broadcast_to(kappa_rows(labels_in[3, bx])[0:1], (cy, nz))
            below = jnp.where(has[2], south_row, plane)
            above = jnp.where(has[3], north_row, plane)
            c_south.append(0.5 * (plane + jnp.where(row_j == 0, below, pltpu.roll(plane, 1, 0))))
            c_north.append(0.5 * (plane + jnp.where(row_j == cy - 1, above, pltpu.roll(plane, cy - 1, 0))))

        def x_face(i):
            left = west_k if i == 0 else kappa[(i - 1) // BLOCK]
            right = east_k if i == cx else kappa[i // BLOCK]
            return left if left is right else 0.5 * (left + right)

        faces = {}
        for i in range(cx + 1):
            key = (min(max(i - 1, -1), cx) // BLOCK, i // BLOCK)
            if key not in faces:
                faces[key] = x_face(i)
        c_x = [faces[((i - 1) // BLOCK if i else -1, i // BLOCK)] for i in range(cx + 1)]

        zero = jnp.zeros((cy, nz), f32)
        loc_south = [jnp.where(row_j == 0, 0.0, c) for c in c_south]
        loc_north = [jnp.where(row_j == cy - 1, 0.0, c) for c in c_north]
        loc_below = [jnp.where(lane_k == 0, 0.0, c) for c in c_below]
        loc_above = [jnp.where(lane_k == nz - 1, 0.0, c) for c in c_above]
        rob_y = p_y * (inside[2] * (row_j == 0).astype(f32) + inside[3] * (row_j == cy - 1).astype(f32))
        known = {}

        def plane_terms(i):
            bx = i // BLOCK
            key = (bx, i % BLOCK == 0, i % BLOCK == BLOCK - 1)
            if key not in known:
                total = reaction + c_x[i] + c_x[i + 1] + c_south[bx] + c_north[bx] + c_below[bx] + c_above[bx]
                local = total + rob_y
                if i == 0:
                    local = local + p_x * inside[0]
                if i == cx - 1:
                    local = local + p_x * inside[1]
                inv = 1.0 / local
                west = zero if i == 0 else c_x[i] * inv
                east = zero if i == cx - 1 else c_x[i + 1] * inv
                known[key] = (
                    total, inv, west, east, loc_south[bx] * inv, loc_north[bx] * inv,
                    loc_below[bx] * inv, loc_above[bx] * inv,
                )
            return known[key]

        for h in range(half):
            lo, hi = plane_terms(2 * h), plane_terms(2 * h + 1)
            diag_s[0, h] = lo[0]
            diag_s[1, h] = hi[0]
            for colour in range(2):
                low = even if colour == 0 else jnp.logical_not(even)
                coef[colour, 0, h] = jnp.where(low, lo[3], hi[2])
                coef[colour, 1, h] = jnp.where(low, lo[2], hi[3])
                for item in range(4):
                    coef[colour, 2 + item, h] = jnp.where(low, lo[4 + item], hi[4 + item])
                coef[colour, 6, h] = jnp.where(low, lo[1], hi[1])

        def stacked(planes):
            return jnp.stack(planes, 0)

        def by_block(planes, parity):
            return stacked([planes[(2 * h + parity) // BLOCK] for h in range(half)])

        even3 = jnp.broadcast_to(even[None], (half, cy, nz))

        def packed(pair):
            return jnp.where(even3, pair[0], pair[1]), jnp.where(even3, pair[1], pair[0])

        def up(v):
            return jnp.concatenate([v[1:], v[:1]], 0)

        def down(v):
            return jnp.concatenate([v[-1:], v[:-1]], 0)

        def coupling(other, colour):
            if colour == 0:
                across = jnp.where(even3, down(other), up(other))
            else:
                across = jnp.where(even3, up(other), down(other))
            total = coef[colour, 0] * other + coef[colour, 1] * across
            total = total + coef[colour, 2] * pltpu.roll(other, 1, 1)
            total = total + coef[colour, 3] * pltpu.roll(other, cy - 1, 1)
            total = total + coef[colour, 4] * pltpu.roll(other, 1, 2)
            return total + coef[colour, 5] * pltpu.roll(other, nz - 1, 2)

        def relax(red, black, source):
            scaled = packed(source)
            scaled = (scaled[0] * coef[0, 6], scaled[1] * coef[1, 6])
            for sweep in range(SWEEPS):
                red = scaled[0] if black is None else scaled[0] + coupling(black, 0)
                black = scaled[1] + coupling(red, 1)
            return red, black

        right = tuple(stacked([rhs[2 * h + parity] for h in range(half)]) for parity in range(2))

        def misfit(u):
            result = []
            for parity in range(2):
                mine, other = u[parity], u[1 - parity]
                faces_w = stacked([zero if 2 * h + parity == 0 else c_x[2 * h + parity] for h in range(half)])
                faces_e = stacked(
                    [zero if 2 * h + parity == cx - 1 else c_x[2 * h + parity + 1] for h in range(half)]
                )
                west = down(other) if parity == 0 else other
                east = other if parity == 0 else up(other)
                total = right[parity] - diag_s[parity] * mine + faces_w * west + faces_e * east
                total = total + by_block(loc_south, parity) * pltpu.roll(mine, 1, 1)
                total = total + by_block(loc_north, parity) * pltpu.roll(mine, cy - 1, 1)
                total = total + by_block(loc_below, parity) * pltpu.roll(mine, 1, 2)
                total = total + by_block(loc_above, parity) * pltpu.roll(mine, nz - 1, 2)
                result.append(total)
            return result

        xi = [(i + 0.5) / cx for i in range(cx)]
        eta = (row_j.astype(f32) + 0.5) / cy
        eta_first, eta_last = 0.5 / cy, (cy - 0.5) / cy

        def weigh_x(pair):
            lows, highs = None, None
            for i in range(cx):
                plane = pair[i % 2][i // 2]
                low, high = (1.0 - xi[i]) * plane, xi[i] * plane
                lows = low if lows is None else lows + low
                highs = high if highs is None else highs + high
            return lows, highs

        win_row = lax.broadcasted_iota(jnp.int32, (16, count), 0)
        win_lane = lax.broadcasted_iota(jnp.int32, (16, count), 1)
        point_w = w + win_row // 4 - 1
        point_n = n + win_row % 4 - 1
        point_ok = (point_w >= 0) & (point_w < wide) & (point_n >= 0) & (point_n < narrow)
        point = jnp.where(point_ok, point_w * narrow + point_n, -1)
        at_point = point == win_lane
        slot_row = lax.broadcasted_iota(jnp.int32, (16, nz), 0)

        def edge_coef(planes, parity, row):
            return stacked([planes[(2 * h + parity) // BLOCK][row : row + 1] for h in range(half)])

        south_c = [edge_coef(c_south, parity, 0) * inside[2] for parity in range(2)]
        north_c = [edge_coef(c_north, parity, cy - 1) * inside[3] for parity in range(2)]
        west_c = c_x[0] * inside[0]
        east_c = c_x[cx] * inside[1]

        def restrict(u):
            low, high = weigh_x(misfit(u))
            out_w = west_c * u[0][0]
            out_e = east_c * u[1][half - 1]
            sums = {
                -1: (1.0 - xi[-1]) * out_w,
                0: low + xi[-1] * out_w,
                1: high + (1.0 - xi[0]) * out_e,
                2: xi[0] * out_e,
            }
            out_s = weigh_x([south_c[parity] * u[parity][:, 0:1] for parity in range(2)])
            out_n = weigh_x([north_c[parity] * u[parity][:, cy - 1 : cy] for parity in range(2)])
            table = jnp.zeros((16, nz), f32)
            for a in range(-1, 3):
                near = jnp.sum(sums[a] * (1.0 - eta), 0, keepdims=True)
                away = jnp.sum(sums[a] * eta, 0, keepdims=True)
                entries = {0: near, 1: away}
                if a in (0, 1):
                    entries[-1] = (1.0 - eta_last) * out_s[a]
                    entries[0] = near + eta_last * out_s[a]
                    entries[1] = away + (1.0 - eta_first) * out_n[a]
                    entries[2] = eta_first * out_n[a]
                for b, entry in entries.items():
                    table = jnp.where(slot_row == slot_at(a, b), jnp.broadcast_to(entry, (16, nz)), table)
            summed = jnp.sum(table, 1, keepdims=True)
            return jnp.sum(jnp.where(at_point, summed, 0.0), 0, keepdims=True)

        def face_copy(turn, side):
            dw, dn = SIDES[side]
            if side < 2:
                source, target = x_out.at[turn, side], x_in.at[turn, side ^ 1]
            else:
                source, target = y_out.at[turn, side - 2], y_in.at[turn, (side ^ 1) - 2]
            return pltpu.make_async_remote_copy(
                src_ref=source, dst_ref=target,
                send_sem=face_send.at[turn, side], recv_sem=face_recv.at[turn, side ^ 1],
                device_id=(w + dw, n + dn), device_id_type=MESH,
            )

        def face_arrival(turn, side):
            dw, dn = SIDES[side]
            if side < 2:
                source, target = x_out.at[turn, side], x_in.at[turn, side]
            else:
                source, target = y_out.at[turn, side - 2], y_in.at[turn, side - 2]
            return pltpu.make_async_remote_copy(
                src_ref=source, dst_ref=target,
                send_sem=face_send.at[turn, side], recv_sem=face_recv.at[turn, side],
                device_id=(w + dw, n + dn), device_id_type=MESH,
            )

        def gather_all(turn):
            return pltpu.make_async_remote_copy(
                src_ref=gathered.at[turn, pl.ds(0, count - 1)], dst_ref=gathered.at[turn, pl.ds(0, count - 1)],
                send_sem=gather_send.at[turn], recv_sem=gather_recv.at[turn],
                device_id=peer(1), device_id_type=MESH,
            )

        next_stage()
        red = black = None
        source = right
        for turn in range(ITERS):
            red, black = relax(red, black, source)
            u = [jnp.where(even3, red, black), jnp.where(even3, black, red)]
            x_out[turn, 0] = u[0][0]
            x_out[turn, 1] = u[1][half - 1]
            for parity in range(2):
                y_out[turn, 0, pl.ds(parity * half, half)] = u[parity][:, 0:1]
                y_out[turn, 1, pl.ds(parity * half, half)] = u[parity][:, cy - 1 : cy]
            for side in range(4):
                @pl.when(has[side])
                def _(turn=turn, side=side):
                    face_copy(turn, side).start()
            gathered[turn, me] = restrict(u)

            def scatter(step, carry, turn=turn):
                pltpu.make_async_remote_copy(
                    src_ref=gathered.at[turn, me], dst_ref=gathered.at[turn, me],
                    send_sem=gather_send.at[turn], recv_sem=gather_recv.at[turn],
                    device_id=peer(step), device_id_type=MESH,
                ).start()
                return carry

            while next_stage():
                pass
            lax.fori_loop(1, count, scatter, 0)
            if turn == 0:
                for a, b in far:
                    @pl.when(on_grid(-a, -b))
                    def _(a=a, b=b):
                        row_copy(a, b).start()
            for side in range(4):
                @pl.when(has[side])
                def _(turn=turn, side=side):
                    face_arrival(turn, side).wait_recv()
            if turn == 0:
                for a, b in far:
                    @pl.when(on_grid(a, b))
                    def _(a=a, b=b):
                        row_copy(a, b).wait_recv()
            gather_all(turn).wait_recv()
            load = jnp.sum(gathered[turn], 0)
            value = {}
            for a, b in SLOTS:
                value[a, b] = jnp.sum(window[slot_at(a, b)] * load, 1, keepdims=True)

            along = {a: value[a, 0] * (1.0 - eta) + value[a, 1] * eta for a in range(-1, 3)}
            u = [
                u[parity]
                + stacked(
                    [
                        (1.0 - xi[2 * h + parity]) * along[0] + xi[2 * h + parity] * along[1]
                        for h in range(half)
                    ]
                )
                for parity in range(2)
            ]
            west_u = x_in[turn, 0] + (1.0 - xi[-1]) * along[-1] + xi[-1] * along[0]
            east_u = x_in[turn, 1] + (1.0 - xi[0]) * along[1] + xi[0] * along[2]
            under = [value[a, -1] * (1.0 - eta_last) + value[a, 0] * eta_last for a in (0, 1)]
            over = [value[a, 1] * (1.0 - eta_first) + value[a, 2] * eta_first for a in (0, 1)]

            def edge(base, ends, parity):
                return base + stacked(
                    [
                        jnp.broadcast_to(
                            (1.0 - xi[2 * h + parity]) * ends[0] + xi[2 * h + parity] * ends[1], (1, nz)
                        )
                        for h in range(half)
                    ]
                )

            south_u = [edge(y_in[turn, 0, pl.ds(parity * half, half)], under, parity) for parity in range(2)]
            north_u = [edge(y_in[turn, 1, pl.ds(parity * half, half)], over, parity) for parity in range(2)]
            out_x = [west_c * west_u, east_c * east_u]
            out_y = [[south_c[parity] * south_u[parity] for parity in range(2)],
                     [north_c[parity] * north_u[parity] for parity in range(2)]]
            last = turn + 1 == ITERS
            if not last:
                out_x[0] = out_x[0] + (inside[0] * p_x) * u[0][0]
                out_x[1] = out_x[1] + (inside[1] * p_x) * u[1][half - 1]
                for parity in range(2):
                    out_y[0][parity] = out_y[0][parity] + (inside[2] * p_y) * u[parity][:, 0:1]
                    out_y[1][parity] = out_y[1][parity] + (inside[3] * p_y) * u[parity][:, cy - 1 : cy]
            base = misfit(u) if last else right
            row3 = jnp.broadcast_to(row_j[None], (half, cy, nz))
            total = []
            for parity in range(2):
                ends = jnp.where(row3 == 0, jnp.broadcast_to(out_y[0][parity], row3.shape), 0.0)
                ends = jnp.where(row3 == cy - 1, jnp.broadcast_to(out_y[1][parity], row3.shape), ends)
                total.append(base[parity] + ends)
            total[0] = jnp.concatenate([total[0][:1] + out_x[0][None], total[0][1:]], 0)
            total[1] = jnp.concatenate([total[1][:-1], total[1][-1:] + out_x[1][None]], 0)
            if last:
                for i in range(cx):
                    sol_ref[i] = u[i % 2][i // 2].astype(jnp.bfloat16)
                    res_ref[i] = total[i % 2][i // 2].astype(jnp.bfloat16)
            else:
                source = total
                red, black = packed(u)

        for side in range(4):
            @pl.when(has[side])
            def _(side=side):
                label_copy(side).wait_send()
                for turn in range(ITERS):
                    face_copy(turn, side).wait_send()
        for a, b in far:
            @pl.when(on_grid(-a, -b))
            def _(a=a, b=b):
                row_copy(a, b).wait_send()
        for turn in range(ITERS):
            gather_all(turn).wait_send()

    scratch = [
        pltpu.SMEM(tables[0], f32),
        pltpu.SMEM(tables[1], f32),
        pltpu.SMEM(tables[2], jnp.int32),
        pltpu.VMEM(shape, f32),
        pltpu.VMEM(blocks, jnp.int32),
        pltpu.VMEM((4,) + blocks, jnp.int32),
        pltpu.VMEM((16, 1, count), f32),
        pltpu.VMEM((ITERS, count, 1, count), f32),
        pltpu.VMEM((ITERS, 2, cy, nz), f32),
        pltpu.VMEM((ITERS, 2, cy, nz), f32),
        pltpu.VMEM((ITERS, 2, cx, 1, nz), f32),
        pltpu.VMEM((ITERS, 2, cx, 1, nz), f32),
        pltpu.VMEM((2, 7, half, cy, nz), f32),
        pltpu.VMEM((2, half, cy, nz), f32),
        pltpu.SemaphoreType.DMA((6,)),
        pltpu.SemaphoreType.DMA((4,)),
        pltpu.SemaphoreType.DMA((4,)),
        pltpu.SemaphoreType.DMA((16,)),
        pltpu.SemaphoreType.DMA((16,)),
        pltpu.SemaphoreType.DMA((ITERS, 4)),
        pltpu.SemaphoreType.DMA((ITERS, 4)),
        pltpu.SemaphoreType.DMA((ITERS,)),
        pltpu.SemaphoreType.DMA((ITERS,)),
        pltpu.SemaphoreType.REGULAR((max(1, len(bits)),)),
    ]
    return kernel, scratch


def solution(mesh):
    wide, narrow = mesh.shape["wide"], mesh.shape["narrow"]

    def body(right_side, labels, material_table, robin_table, robin_index, coarse_rows):
        shape = right_side.shape
        kernel, scratch = make_kernel(
            wide, narrow, shape, labels.shape, (material_table.shape, robin_table.shape, robin_index.shape)
        )
        anywhere = pl.BlockSpec(memory_space=pl.ANY)
        vectors = pl.BlockSpec(memory_space=pltpu.VMEM)
        return pl.pallas_call(
            kernel,
            out_shape=(pltpu.VMEM(shape, jnp.bfloat16),) * 2,
            in_specs=[anywhere] * 6,
            out_specs=(vectors, vectors),
            scratch_shapes=scratch,
            compiler_params=pltpu.CompilerParams(collective_id=0, has_side_effects=True),
        )(right_side, labels, material_table, robin_table, robin_index, coarse_rows)

    cells = P("wide", "narrow", None)
    return jax.shard_map(
        body,
        mesh=mesh,
        in_specs=(cells, cells, P(), P(), cells, P(("wide", "narrow"), None)),
        out_specs=(cells, cells),
        check_vma=False,
    )
```

```python
import jax
import jax.numpy as jnp
from jax import lax
from jax.experimental import pallas as pl
from jax.experimental.pallas import tpu as pltpu
from jax.sharding import PartitionSpec as P

BLOCK = 8
SWEEPS = 4
ITERS = 2
reaction = 1.0
MESH = pl.DeviceIdType.MESH
SIDES = ((-1, 0), (1, 0), (0, -1), (0, 1))
SLOTS = [(a, b) for a in range(-1, 3) for b in range(-1, 3) if a in (0, 1) or b in (0, 1)]


def slot_at(a, b):
    return 4 * (a + 1) + (b + 1)


def make_kernel(wide, narrow, shape, blocks, tables):
    cx, cy, nz = shape
    half = cx // 2
    count = wide * narrow
    paired = False
    bits = [(1 << k, 0) for k in reversed(range(wide.bit_length() - 1))]
    bits += [(0, 1 << k) for k in range(narrow.bit_length() - 1)]
    others = [(dw, dn) for dw in range(wide) for dn in range(narrow) if dw or dn]
    others.sort(key=lambda by: (abs(by[0] - wide // 2), -by[1]))
    blocks_x, blocks_y, blocks_z = blocks
    f32 = jnp.float32

    def kernel(
        rhs_hbm, labels_hbm, material_hbm, robin_hbm, index_hbm, rows_hbm,
        sol_ref, res_ref,
        material, robin_table, robin_index, rhs, labels, labels_in, window, gathered, x_out, x_in, y_out, y_in, coef, diag_s,
        local_sem, label_send, label_recv, row_send, row_recv,
        face_send, face_recv, gather_send, gather_recv, known_sem,
    ):
        w = lax.axis_index("wide")
        n = lax.axis_index("narrow")
        me = w * narrow + n
        loads = [
            pltpu.make_async_copy(labels_hbm, labels, local_sem.at[0]),
            pltpu.make_async_copy(rows_hbm, window.at[slot_at(0, 0)], local_sem.at[1]),
            pltpu.make_async_copy(rhs_hbm, rhs, local_sem.at[2]),
            pltpu.make_async_copy(material_hbm, material, local_sem.at[3]),
            pltpu.make_async_copy(robin_hbm, robin_table, local_sem.at[4]),
            pltpu.make_async_copy(index_hbm, robin_index, local_sem.at[5]),
        ]
        labels_in[...] = jnp.zeros_like(labels_in)
        x_in[...] = jnp.zeros_like(x_in)
        y_in[...] = jnp.zeros_like(y_in)
        for a, b in SLOTS:
            if (a, b) != (0, 0):
                window[slot_at(a, b)] = jnp.zeros_like(window[slot_at(a, b)])
        for load in loads:
            load.start()
        barrier = pltpu.get_barrier_semaphore()

        def peer(step):
            flat = me + step
            flat = jnp.where(flat >= count, flat - count, flat)
            return (flat // narrow, flat % narrow)

        has = [w > 0, w < wide - 1, n > 0, n < narrow - 1]

        def flipped(at, bit):
            return at + bit - 2 * bit * (at // bit % 2) if bit else at

        def partner(stage):
            return (flipped(w, bits[stage][0]), flipped(n, bits[stage][1]))

        def signal(sem, target):
            pl.semaphore_signal(sem, inc=1, device_id=target, device_id_type=MESH)

        if paired:
            for side in range(4):
                @pl.when(has[side])
                def _(side=side):
                    signal(barrier, (w + SIDES[side][0], n + SIDES[side][1]))
            greeted = sum(jnp.where(flag, 1, 0) for flag in has) + len(bits)
            for stage in range(len(bits)):
                signal(barrier, partner(stage))
        else:
            for dw, dn in others:
                signal(barrier, ((w + dw) % wide, (n + dn) % narrow))
            greeted = len(others)
        stages = iter(range(len(bits)))

        def begin_stage():
            signal(known_sem.at[0], partner(0))

        def next_stage():
            stage = next(stages, None)
            if paired and stage is not None:
                pl.semaphore_wait(known_sem.at[stage], 1)
                if stage + 1 < len(bits):
                    signal(known_sem.at[stage + 1], partner(stage + 1))
            return stage is not None

        inside = [jnp.where(flag, 1.0, 0.0).astype(f32) for flag in has]
        spread = (
            lax.broadcasted_iota(jnp.int32, (blocks_z, nz), 1) // BLOCK
            == lax.broadcasted_iota(jnp.int32, (blocks_z, nz), 0)
        ).astype(f32)
        row_j = lax.broadcasted_iota(jnp.int32, (cy, nz), 0)
        lane_k = lax.broadcasted_iota(jnp.int32, (cy, nz), 1)
        even = (row_j + lane_k) % 2 == 0

        def kappa_rows(label_rows):
            wide_rows = jnp.dot(label_rows.astype(f32), spread, preferred_element_type=f32)
            found = jnp.zeros_like(wide_rows)
            for entry in range(material.shape[0]):
                found = jnp.where(wide_rows == float(entry), material[entry], found)
            return found

        def plane_of(rows):
            plane = jnp.broadcast_to(rows[blocks_y - 1 : blocks_y], (cy, nz))
            for at in range(blocks_y - 2, -1, -1):
                plane = jnp.where(row_j < (at + 1) * BLOCK, jnp.broadcast_to(rows[at : at + 1], (cy, nz)), plane)
            return plane

        for at in (0, 1, 3, 4, 5):
            loads[at].wait()
        p_x = robin_table[robin_index[0, 0, 0]]
        p_y = robin_table[robin_index[0, 0, 1]]

        kappa = [plane_of(kappa_rows(labels[bx])) for bx in range(blocks_x)]
        c_below, c_above = [], []
        for plane in kappa:
            c_below.append(0.5 * (plane + jnp.where(lane_k == 0, plane, pltpu.roll(plane, 1, 1))))
            c_above.append(0.5 * (plane + jnp.where(lane_k == nz - 1, plane, pltpu.roll(plane, nz - 1, 1))))

        pl.semaphore_wait(barrier, greeted)

        def label_copy(side):
            dw, dn = SIDES[side]
            return pltpu.make_async_remote_copy(
                src_ref=labels, dst_ref=labels_in.at[side ^ 1],
                send_sem=label_send.at[side], recv_sem=label_recv.at[side ^ 1],
                device_id=(w + dw, n + dn), device_id_type=MESH,
            )

        def label_arrival(side):
            dw, dn = SIDES[side]
            return pltpu.make_async_remote_copy(
                src_ref=labels, dst_ref=labels_in.at[side],
                send_sem=label_send.at[side], recv_sem=label_recv.at[side],
                device_id=(w + dw, n + dn), device_id_type=MESH,
            )

        for side in range(4):
            @pl.when(has[side])
            def _(side=side):
                label_copy(side).start()

        def on_grid(a, b):
            return (w + a >= 0) & (w + a < wide) & (n + b >= 0) & (n + b < narrow)

        def row_copy(a, b):
            slot = slot_at(a, b)
            return pltpu.make_async_remote_copy(
                src_ref=window.at[slot_at(0, 0)], dst_ref=window.at[slot],
                send_sem=row_send.at[slot], recv_sem=row_recv.at[slot],
                device_id=(w - a, n - b), device_id_type=MESH,
            )

        far = [(a, b) for a, b in SLOTS if (a, b) != (0, 0) and abs(a) < wide and abs(b) < narrow]
        for a, b in far:
            @pl.when(on_grid(-a, -b))
            def _(a=a, b=b):
                row_copy(a, b).start()

        if paired and bits:
            begin_stage()
            next_stage()
            next_stage()
        loads[2].wait()
        for side in range(4):
            @pl.when(has[side])
            def _(side=side):
                label_arrival(side).wait_recv()

        next_stage()
        west_k = jnp.where(has[0], plane_of(kappa_rows(labels_in[0, blocks_x - 1])), kappa[0])
        east_k = jnp.where(has[1], plane_of(kappa_rows(labels_in[1, 0])), kappa[-1])
        c_south, c_north = [], []
        for bx in range(blocks_x):
            plane = kappa[bx]
            south_row = jnp.broadcast_to(kappa_rows(labels_in[2, bx])[blocks_y - 1 : blocks_y], (cy, nz))
            north_row = jnp.broadcast_to(kappa_rows(labels_in[3, bx])[0:1], (cy, nz))
            below = jnp.where(has[2], south_row, plane)
            above = jnp.where(has[3], north_row, plane)
            c_south.append(0.5 * (plane + jnp.where(row_j == 0, below, pltpu.roll(plane, 1, 0))))
            c_north.append(0.5 * (plane + jnp.where(row_j == cy - 1, above, pltpu.roll(plane, cy - 1, 0))))

        def x_face(i):
            left = west_k if i == 0 else kappa[(i - 1) // BLOCK]
            right = east_k if i == cx else kappa[i // BLOCK]
            return left if left is right else 0.5 * (left + right)

        faces = {}
        for i in range(cx + 1):
            key = (min(max(i - 1, -1), cx) // BLOCK, i // BLOCK)
            if key not in faces:
                faces[key] = x_face(i)
        c_x = [faces[((i - 1) // BLOCK if i else -1, i // BLOCK)] for i in range(cx + 1)]

        zero = jnp.zeros((cy, nz), f32)
        loc_south = [jnp.where(row_j == 0, 0.0, c) for c in c_south]
        loc_north = [jnp.where(row_j == cy - 1, 0.0, c) for c in c_north]
        loc_below = [jnp.where(lane_k == 0, 0.0, c) for c in c_below]
        loc_above = [jnp.where(lane_k == nz - 1, 0.0, c) for c in c_above]
        rob_y = p_y * (inside[2] * (row_j == 0).astype(f32) + inside[3] * (row_j == cy - 1).astype(f32))
        known = {}

        def plane_terms(i):
            bx = i // BLOCK
            key = (bx, i % BLOCK == 0, i % BLOCK == BLOCK - 1)
            if key not in known:
                total = reaction + c_x[i] + c_x[i + 1] + c_south[bx] + c_north[bx] + c_below[bx] + c_above[bx]
                local = total + rob_y
                if i == 0:
                    local = local + p_x * inside[0]
                if i == cx - 1:
                    local = local + p_x * inside[1]
                inv = 1.0 / local
                west = zero if i == 0 else c_x[i] * inv
                east = zero if i == cx - 1 else c_x[i + 1] * inv
                known[key] = (
                    total, inv, west, east, loc_south[bx] * inv, loc_north[bx] * inv,
                    loc_below[bx] * inv, loc_above[bx] * inv,
                )
            return known[key]

        for h in range(half):
            lo, hi = plane_terms(2 * h), plane_terms(2 * h + 1)
            diag_s[0, h] = lo[0]
            diag_s[1, h] = hi[0]
            for colour in range(2):
                low = even if colour == 0 else jnp.logical_not(even)
                coef[colour, 0, h] = jnp.where(low, lo[3], hi[2])
                coef[colour, 1, h] = jnp.where(low, lo[2], hi[3])
                for item in range(4):
                    coef[colour, 2 + item, h] = jnp.where(low, lo[4 + item], hi[4 + item])
                coef[colour, 6, h] = jnp.where(low, lo[1], hi[1])

        def stacked(planes):
            return jnp.stack(planes, 0)

        def by_block(planes, parity):
            return stacked([planes[(2 * h + parity) // BLOCK] for h in range(half)])

        even3 = jnp.broadcast_to(even[None], (half, cy, nz))

        def packed(pair):
            return jnp.where(even3, pair[0], pair[1]), jnp.where(even3, pair[1], pair[0])

        def up(v):
            return jnp.concatenate([v[1:], v[:1]], 0)

        def down(v):
            return jnp.concatenate([v[-1:], v[:-1]], 0)

        def coupling(other, colour):
            if colour == 0:
                across = jnp.where(even3, down(other), up(other))
            else:
                across = jnp.where(even3, up(other), down(other))
            total = coef[colour, 0] * other + coef[colour, 1] * across
            total = total + coef[colour, 2] * pltpu.roll(other, 1, 1)
            total = total + coef[colour, 3] * pltpu.roll(other, cy - 1, 1)
            total = total + coef[colour, 4] * pltpu.roll(other, 1, 2)
            return total + coef[colour, 5] * pltpu.roll(other, nz - 1, 2)

        def relax(red, black, source):
            scaled = packed(source)
            scaled = (scaled[0] * coef[0, 6], scaled[1] * coef[1, 6])
            for sweep in range(SWEEPS):
                red = scaled[0] if black is None else scaled[0] + coupling(black, 0)
                black = scaled[1] + coupling(red, 1)
            return red, black

        right = tuple(stacked([rhs[2 * h + parity] for h in range(half)]) for parity in range(2))

        def misfit(u):
            result = []
            for parity in range(2):
                mine, other = u[parity], u[1 - parity]
                faces_w = stacked([zero if 2 * h + parity == 0 else c_x[2 * h + parity] for h in range(half)])
                faces_e = stacked(
                    [zero if 2 * h + parity == cx - 1 else c_x[2 * h + parity + 1] for h in range(half)]
                )
                west = down(other) if parity == 0 else other
                east = other if parity == 0 else up(other)
                total = right[parity] - diag_s[parity] * mine + faces_w * west + faces_e * east
                total = total + by_block(loc_south, parity) * pltpu.roll(mine, 1, 1)
                total = total + by_block(loc_north, parity) * pltpu.roll(mine, cy - 1, 1)
                total = total + by_block(loc_below, parity) * pltpu.roll(mine, 1, 2)
                total = total + by_block(loc_above, parity) * pltpu.roll(mine, nz - 1, 2)
                result.append(total)
            return result

        xi = [(i + 0.5) / cx for i in range(cx)]
        eta = (row_j.astype(f32) + 0.5) / cy
        eta_first, eta_last = 0.5 / cy, (cy - 0.5) / cy

        def weigh_x(pair):
            lows, highs = None, None
            for i in range(cx):
                plane = pair[i % 2][i // 2]
                low, high = (1.0 - xi[i]) * plane, xi[i] * plane
                lows = low if lows is None else lows + low
                highs = high if highs is None else highs + high
            return lows, highs

        win_row = lax.broadcasted_iota(jnp.int32, (16, count), 0)
        win_lane = lax.broadcasted_iota(jnp.int32, (16, count), 1)
        point_w = w + win_row // 4 - 1
        point_n = n + win_row % 4 - 1
        point_ok = (point_w >= 0) & (point_w < wide) & (point_n >= 0) & (point_n < narrow)
        point = jnp.where(point_ok, point_w * narrow + point_n, -1)
        at_point = point == win_lane
        slot_row = lax.broadcasted_iota(jnp.int32, (16, nz), 0)

        def edge_coef(planes, parity, row):
            return stacked([planes[(2 * h + parity) // BLOCK][row : row + 1] for h in range(half)])

        south_c = [edge_coef(c_south, parity, 0) * inside[2] for parity in range(2)]
        north_c = [edge_coef(c_north, parity, cy - 1) * inside[3] for parity in range(2)]
        west_c = c_x[0] * inside[0]
        east_c = c_x[cx] * inside[1]

        def restrict(u):
            low, high = weigh_x(misfit(u))
            out_w = west_c * u[0][0]
            out_e = east_c * u[1][half - 1]
            sums = {
                -1: (1.0 - xi[-1]) * out_w,
                0: low + xi[-1] * out_w,
                1: high + (1.0 - xi[0]) * out_e,
                2: xi[0] * out_e,
            }
            out_s = weigh_x([south_c[parity] * u[parity][:, 0:1] for parity in range(2)])
            out_n = weigh_x([north_c[parity] * u[parity][:, cy - 1 : cy] for parity in range(2)])
            table = jnp.zeros((16, nz), f32)
            for a in range(-1, 3):
                near = jnp.sum(sums[a] * (1.0 - eta), 0, keepdims=True)
                away = jnp.sum(sums[a] * eta, 0, keepdims=True)
                entries = {0: near, 1: away}
                if a in (0, 1):
                    entries[-1] = (1.0 - eta_last) * out_s[a]
                    entries[0] = near + eta_last * out_s[a]
                    entries[1] = away + (1.0 - eta_first) * out_n[a]
                    entries[2] = eta_first * out_n[a]
                for b, entry in entries.items():
                    table = jnp.where(slot_row == slot_at(a, b), jnp.broadcast_to(entry, (16, nz)), table)
            summed = jnp.sum(table, 1, keepdims=True)
            return jnp.sum(jnp.where(at_point, summed, 0.0), 0, keepdims=True)

        def face_copy(turn, side):
            dw, dn = SIDES[side]
            if side < 2:
                source, target = x_out.at[turn, side], x_in.at[turn, side ^ 1]
            else:
                source, target = y_out.at[turn, side - 2], y_in.at[turn, (side ^ 1) - 2]
            return pltpu.make_async_remote_copy(
                src_ref=source, dst_ref=target,
                send_sem=face_send.at[turn, side], recv_sem=face_recv.at[turn, side ^ 1],
                device_id=(w + dw, n + dn), device_id_type=MESH,
            )

        def face_arrival(turn, side):
            dw, dn = SIDES[side]
            if side < 2:
                source, target = x_out.at[turn, side], x_in.at[turn, side]
            else:
                source, target = y_out.at[turn, side - 2], y_in.at[turn, side - 2]
            return pltpu.make_async_remote_copy(
                src_ref=source, dst_ref=target,
                send_sem=face_send.at[turn, side], recv_sem=face_recv.at[turn, side],
                device_id=(w + dw, n + dn), device_id_type=MESH,
            )

        def gather_all(turn):
            return pltpu.make_async_remote_copy(
                src_ref=gathered.at[turn, pl.ds(0, count - 1)], dst_ref=gathered.at[turn, pl.ds(0, count - 1)],
                send_sem=gather_send.at[turn], recv_sem=gather_recv.at[turn],
                device_id=peer(1), device_id_type=MESH,
            )

        next_stage()
        red = black = None
        source = right
        for turn in range(ITERS):
            red, black = relax(red, black, source)
            u = [jnp.where(even3, red, black), jnp.where(even3, black, red)]
            x_out[turn, 0] = u[0][0]
            x_out[turn, 1] = u[1][half - 1]
            for parity in range(2):
                y_out[turn, 0, pl.ds(parity * half, half)] = u[parity][:, 0:1]
                y_out[turn, 1, pl.ds(parity * half, half)] = u[parity][:, cy - 1 : cy]
            for side in range(4):
                @pl.when(has[side])
                def _(turn=turn, side=side):
                    face_copy(turn, side).start()
            gathered[turn, me] = restrict(u)

            def scatter(step, carry, turn=turn):
                pltpu.make_async_remote_copy(
                    src_ref=gathered.at[turn, me], dst_ref=gathered.at[turn, me],
                    send_sem=gather_send.at[turn], recv_sem=gather_recv.at[turn],
                    device_id=peer(step), device_id_type=MESH,
                ).start()
                return carry

            while next_stage():
                pass
            lax.fori_loop(1, count, scatter, 0, unroll=count <= 64)
            for side in range(4):
                @pl.when(has[side])
                def _(turn=turn, side=side):
                    face_arrival(turn, side).wait_recv()
            if turn == 0:
                for a, b in far:
                    @pl.when(on_grid(a, b))
                    def _(a=a, b=b):
                        row_copy(a, b).wait_recv()
            gather_all(turn).wait_recv()
            load = jnp.sum(gathered[turn], 0)
            value = {}
            for a, b in SLOTS:
                value[a, b] = jnp.sum(window[slot_at(a, b)] * load, 1, keepdims=True)

            along = {a: value[a, 0] * (1.0 - eta) + value[a, 1] * eta for a in range(-1, 3)}
            u = [
                u[parity]
                + stacked(
                    [
                        (1.0 - xi[2 * h + parity]) * along[0] + xi[2 * h + parity] * along[1]
                        for h in range(half)
                    ]
                )
                for parity in range(2)
            ]
            west_u = x_in[turn, 0] + (1.0 - xi[-1]) * along[-1] + xi[-1] * along[0]
            east_u = x_in[turn, 1] + (1.0 - xi[0]) * along[1] + xi[0] * along[2]
            under = [value[a, -1] * (1.0 - eta_last) + value[a, 0] * eta_last for a in (0, 1)]
            over = [value[a, 1] * (1.0 - eta_first) + value[a, 2] * eta_first for a in (0, 1)]

            def edge(base, ends, parity):
                return base + stacked(
                    [
                        jnp.broadcast_to(
                            (1.0 - xi[2 * h + parity]) * ends[0] + xi[2 * h + parity] * ends[1], (1, nz)
                        )
                        for h in range(half)
                    ]
                )

            south_u = [edge(y_in[turn, 0, pl.ds(parity * half, half)], under, parity) for parity in range(2)]
            north_u = [edge(y_in[turn, 1, pl.ds(parity * half, half)], over, parity) for parity in range(2)]
            out_x = [west_c * west_u, east_c * east_u]
            out_y = [[south_c[parity] * south_u[parity] for parity in range(2)],
                     [north_c[parity] * north_u[parity] for parity in range(2)]]
            last = turn + 1 == ITERS
            if not last:
                out_x[0] = out_x[0] + (inside[0] * p_x) * u[0][0]
                out_x[1] = out_x[1] + (inside[1] * p_x) * u[1][half - 1]
                for parity in range(2):
                    out_y[0][parity] = out_y[0][parity] + (inside[2] * p_y) * u[parity][:, 0:1]
                    out_y[1][parity] = out_y[1][parity] + (inside[3] * p_y) * u[parity][:, cy - 1 : cy]
            base = misfit(u) if last else right
            row3 = jnp.broadcast_to(row_j[None], (half, cy, nz))
            total = []
            for parity in range(2):
                ends = jnp.where(row3 == 0, jnp.broadcast_to(out_y[0][parity], row3.shape), 0.0)
                ends = jnp.where(row3 == cy - 1, jnp.broadcast_to(out_y[1][parity], row3.shape), ends)
                total.append(base[parity] + ends)
            total[0] = jnp.concatenate([total[0][:1] + out_x[0][None], total[0][1:]], 0)
            total[1] = jnp.concatenate([total[1][:-1], total[1][-1:] + out_x[1][None]], 0)
            if last:
                for i in range(cx):
                    sol_ref[i] = u[i % 2][i // 2].astype(jnp.bfloat16)
                    res_ref[i] = total[i % 2][i // 2].astype(jnp.bfloat16)
            else:
                source = total
                red, black = packed(u)

        for side in range(4):
            @pl.when(has[side])
            def _(side=side):
                label_copy(side).wait_send()
                for turn in range(ITERS):
                    face_copy(turn, side).wait_send()
        for a, b in far:
            @pl.when(on_grid(-a, -b))
            def _(a=a, b=b):
                row_copy(a, b).wait_send()
        for turn in range(ITERS):
            gather_all(turn).wait_send()

    scratch = [
        pltpu.SMEM(tables[0], f32),
        pltpu.SMEM(tables[1], f32),
        pltpu.SMEM(tables[2], jnp.int32),
        pltpu.VMEM(shape, f32),
        pltpu.VMEM(blocks, jnp.int32),
        pltpu.VMEM((4,) + blocks, jnp.int32),
        pltpu.VMEM((16, 1, count), f32),
        pltpu.VMEM((ITERS, count, 1, count), f32),
        pltpu.VMEM((ITERS, 2, cy, nz), f32),
        pltpu.VMEM((ITERS, 2, cy, nz), f32),
        pltpu.VMEM((ITERS, 2, cx, 1, nz), f32),
        pltpu.VMEM((ITERS, 2, cx, 1, nz), f32),
        pltpu.VMEM((2, 7, half, cy, nz), f32),
        pltpu.VMEM((2, half, cy, nz), f32),
        pltpu.SemaphoreType.DMA((6,)),
        pltpu.SemaphoreType.DMA((4,)),
        pltpu.SemaphoreType.DMA((4,)),
        pltpu.SemaphoreType.DMA((16,)),
        pltpu.SemaphoreType.DMA((16,)),
        pltpu.SemaphoreType.DMA((ITERS, 4)),
        pltpu.SemaphoreType.DMA((ITERS, 4)),
        pltpu.SemaphoreType.DMA((ITERS,)),
        pltpu.SemaphoreType.DMA((ITERS,)),
        pltpu.SemaphoreType.REGULAR((max(1, len(bits)),)),
    ]
    return kernel, scratch


def solution(mesh):
    wide, narrow = mesh.shape["wide"], mesh.shape["narrow"]

    def body(right_side, labels, material_table, robin_table, robin_index, coarse_rows):
        shape = right_side.shape
        kernel, scratch = make_kernel(
            wide, narrow, shape, labels.shape, (material_table.shape, robin_table.shape, robin_index.shape)
        )
        anywhere = pl.BlockSpec(memory_space=pl.ANY)
        vectors = pl.BlockSpec(memory_space=pltpu.VMEM)
        return pl.pallas_call(
            kernel,
            out_shape=(pltpu.VMEM(shape, jnp.bfloat16),) * 2,
            in_specs=[anywhere] * 6,
            out_specs=(vectors, vectors),
            scratch_shapes=scratch,
            compiler_params=pltpu.CompilerParams(collective_id=0, has_side_effects=True),
        )(right_side, labels, material_table, robin_table, robin_index, coarse_rows)

    cells = P("wide", "narrow", None)
    return jax.shard_map(
        body,
        mesh=mesh,
        in_specs=(cells, cells, P(), P(), cells, P(("wide", "narrow"), None)),
        out_specs=(cells, cells),
        check_vma=False,
    )
```
